256 devices in a mesh: grp: 8 (over y, x_lo), ctx: 32 (over z, x_hi, core).
Axes of the slice: x: 4 (x_hi: 2, x_lo: 2; x = x_hi * 2 + x_lo), y: 4, z: 8, core: 2. Of those that a mesh axis runs over, the one named last changes fastest.
Arguments:
- tokens: bfloat16 [8, 2048, 4096], P('grp', 'ctx'), may hold values from -8 to 8
- req_lengths: int32 [8, 8], replicated, may hold values from 1 to 1088, 2048 in all within a row
- req_adapter: int32 [8, 8], replicated, may hold values from 0 to 7
- adapter_slot: int32 [8], replicated, may hold values from 0 to 7, each once
- query_weight: bfloat16 [4096, 4096], P(None, 'grp'), may hold values from -0.109375 to 0.109375
- key_weight: bfloat16 [4096, 1024], P(None, 'grp'), may hold values from -0.109375 to 0.109375
- value_weight: bfloat16 [4096, 1024], P(None, 'grp'), may hold values from -0.09375 to 0.09375
- w_out: bfloat16 [4096, 4096], P('grp'), may hold values from -0.09375 to 0.09375
- down_qkv: bfloat16 [8, 48, 4096], P('grp'), may hold values from -0.09375 to 0.09375
- up_query: bfloat16 [8, 16, 4096], P('grp'), may hold values from -0.59765625 to 0.59765625
- up_kv: bfloat16 [8, 2, 16, 1024], P('grp'), may hold values from -0.59765625 to 0.59765625
- down_out: bfloat16 [8, 16, 4096], P('grp'), may hold values from -0.09375 to 0.09375
- up_out: bfloat16 [8, 16, 4096], P('grp'), may hold values from -0.59765625 to 0.59765625
Outputs:
- mixed: bfloat16 [8, 2048, 4096], P('grp', 'ctx')
The draws below stay inside these ranges and needn't reach their ends.
Inputs may be any that keep to these rules, and one draw needn't show every extreme that they name: `req_lengths`: row b holds the lengths of group b's 8 requests in order; each row sums to 2048 and its longest request has 1088 positions. adapter a's tables stand at slot adapter_slot[a]; every slot is used by one adapter.
All inputs are finite; a program needn't handle non-finite values.
Results may differ from the reference program's by a relative error of at most 0.015.
The reference program's roundings to bfloat16 on the way count: a program that leaves them out, or rounds other values in their place, can miss the bound.
Values may be sent and summed in bfloat16 or wider, within the bound.
A program may use at most 128 MiB of HBM per device.

```python
import math
import jax
import jax.numpy as jnp
import numpy as np
from jax import lax

MODEL_WIDTH = 4096
QH = 32
KVH = 8
HD = 128
ADAPTER_RANK = 16
REQS = 8
GROUPS = 8
SEQ = 2048
ADAPTERS = 8
LONGEST = 1088
N_GRP = 8


def draw_tokens(key, part):
    values = jax.random.truncated_normal(jax.random.fold_in(key, 34), -6.0, 6.0, (GROUPS, SEQ, MODEL_WIDTH), jnp.float32)
    return values.astype(jnp.bfloat16)


def projection_pair(key):
    base = jax.random.truncated_normal(jax.random.fold_in(key, 7002), -6.0, 6.0, (MODEL_WIDTH, QH * HD), jnp.float32) * MODEL_WIDTH ** (-0.5)
    key_part = jax.random.truncated_normal(jax.random.fold_in(key, 7003), -6.0, 6.0, (MODEL_WIDTH, KVH * HD), jnp.float32) * MODEL_WIDTH ** (-0.5)
    return (base, key_part)


def draw_query_weight(key, part):
    return projection_pair(key)[0].astype(jnp.bfloat16)


def draw_key_weight(key, part):
    return projection_pair(key)[1].astype(jnp.bfloat16)


def place_ends(array, rng, least, largest):
    extent = array.shape
    place = [jax.random.randint(jax.random.fold_in(rng, axis), (), 0, extent[axis]) for axis in range(len(extent))]
    array = array.at[tuple(place)].set(least)
    longest = extent.index(max(extent))
    place[longest] = (place[longest] + 1) % extent[longest]
    return array.at[tuple(place)].set(largest)


def level_of(key, dims, cuts, low, largest):
    loudness, own = 1.0, jax.random.fold_in(key, 6)
    for position, blocks in cuts:
        draws = jnp.exp(jax.random.uniform(jax.random.fold_in(own, position), (blocks,), jnp.float32, low / len(cuts), largest / len(cuts)))
        loudness = loudness * jnp.repeat(draws, dims[position] // blocks).reshape([-1 if axis == position else 1 for axis in range(len(dims))])
    return loudness


def split_up(count, total, most, skew):
    weights = [(1 << 20) // math.isqrt(rank ** skew) + 1 for rank in range(2, count + 1)]
    surplus, given = total - most - (count - 1), [1] * (count - 1)
    while surplus > 0:
        candidates = [i for i in range(count - 1) if given[i] < most]
        mass, budget = sum([weights[i] for i in candidates]), surplus
        for i in candidates:
            extra = min(most - given[i], max(1, budget * weights[i] // mass), surplus)
            given[i] = given[i] + extra
            surplus = surplus - extra
    return np.array([most] + given)


def uneven(stream_key, amount, total, bound, skew):
    if amount == 2:
        one = jax.random.randint(stream_key, (), max(1, total - bound), min(bound, total - 1) + 1)
        return jnp.stack([one, total - one])
    tallies = jnp.asarray(split_up(amount, total, bound, skew), jnp.int32)
    twos = (amount - 1) // 2
    giver, sink = tallies[1:1 + 2 * twos:2], tallies[2:2 + 2 * twos:2]
    room = jnp.minimum(giver - 1, bound - sink)
    shifted = jax.random.randint(jax.random.fold_in(stream_key, 1), (twos,), 0, 1 << 20) % (room + 1)
    tallies = tallies.at[1:1 + 2 * twos:2].set(giver - shifted).at[2:2 + 2 * twos:2].set(sink + shifted)
    return tallies[jax.random.permutation(jax.random.fold_in(stream_key, 2), amount)]


def noise(stream_key, shape, width, limit, cuts=(), kind=jnp.bfloat16):
    result = jax.random.normal(stream_key, shape, jnp.float32) * width
    if len(cuts) > 0:
        result = level_of(stream_key, shape, cuts, -0.22, 0.18) * result
    return jnp.clip(result, min=-limit, max=limit).astype(kind)


def setup_inputs(seed: int = 0) -> dict:
    streams_of = jax.random.split(jax.random.key(seed), 14)
    return {
        "tokens": draw_tokens(jax.random.fold_in(streams_of[13], 71), 0),
        "req_lengths": jax.vmap(lambda own: uneven(own, REQS, SEQ, LONGEST, 2))(jax.random.split(streams_of[1], GROUPS)).reshape((GROUPS, REQS)).astype(jnp.int32),
        "req_adapter": place_ends(jax.random.randint(streams_of[2], (GROUPS, REQS), 0, ADAPTERS), jax.random.fold_in(streams_of[2], 1), 0, ADAPTERS - 1).astype(jnp.int32),
        "adapter_slot": jax.random.permutation(streams_of[3], ADAPTERS).astype(jnp.int32),
        "query_weight": draw_query_weight(jax.random.fold_in(streams_of[13], 71), 0),
        "key_weight": draw_key_weight(jax.random.fold_in(streams_of[13], 71), 0),
        "value_weight": noise(streams_of[6], (MODEL_WIDTH, KVH * HD), MODEL_WIDTH ** -0.5, 0.09375, ((1, 8),)),
        "w_out": noise(streams_of[7], (QH * HD, MODEL_WIDTH), (QH * HD) ** -0.5, 0.09375, ((0, 8),)),
        "down_qkv": noise(streams_of[8], (ADAPTERS, 3 * ADAPTER_RANK, MODEL_WIDTH), MODEL_WIDTH ** -0.5, 0.09375, ((0, 8),)),
        "up_query": noise(streams_of[9], (ADAPTERS, ADAPTER_RANK, QH * HD), 0.1, 0.59765625, ((0, 8),)),
        "up_kv": noise(streams_of[10], (ADAPTERS, 2, ADAPTER_RANK, KVH * HD), 0.1, 0.59765625, ((0, 8),)),
        "down_out": noise(streams_of[11], (ADAPTERS, ADAPTER_RANK, QH * HD), (QH * HD) ** -0.5, 0.09375, ((0, 8),)),
        "up_out": noise(streams_of[12], (ADAPTERS, ADAPTER_RANK, MODEL_WIDTH), 0.1, 0.59765625, ((0, 8),)),
    }


ROPE_BASE = 500000.0
ADAPTER_SCALE = 2.0
MASKED_SCORE = -1e+30

def request_info(lengths, adapter_ids, positions):
    req_ends = jnp.cumsum(lengths, axis=-1)
    starts = req_ends - lengths
    segment = lax.optimization_barrier(jnp.sum((req_ends[..., None, :] <= positions[:, None]).astype(jnp.int32), axis=-1))
    req_picks = (segment[..., None] == jnp.arange(lengths.shape[-1], dtype=jnp.int32)).astype(jnp.int32)
    req_begin = lax.optimization_barrier(jnp.sum(req_picks * starts[..., None, :], axis=-1))
    req_owner = lax.optimization_barrier(jnp.sum(req_picks * adapter_ids[..., None, :], axis=-1))
    return (segment, req_begin, req_owner)

def rotate(values, offsets):
    half_width = values.shape[-1] // 2
    frequency = jnp.exp(jnp.arange(half_width, dtype=jnp.float32) * (-2.0 * math.log(ROPE_BASE) / values.shape[-1]))
    angles = offsets[..., None, None] * frequency
    cosine = jnp.cos(angles)
    sine = jnp.sin(angles)
    lower_half = values[..., :half_width]
    upper_half = values[..., half_width:]
    return jnp.concatenate([lower_half * cosine - upper_half * sine, upper_half * cosine + lower_half * sine], axis=-1)

def widen_rows(adapter_middle, adapter_onehot, upward_table):
    masked_scores = adapter_onehot[:, :, None] * adapter_middle[:, None, :]
    flat_rows = masked_scores.reshape(masked_scores.shape[0], upward_table.shape[0] * upward_table.shape[1])
    return jnp.dot(flat_rows, upward_table.reshape(upward_table.shape[0] * upward_table.shape[1], upward_table.shape[2]), preferred_element_type=jnp.float32)

def one_group(input_rows, lengths, adapter_ids, tables):
    down_adapter, up_query_adapter, up_key_adapter, up_value_adapter, downo_ad, up_output_adapter, query_weight, key_weight, value_weight, w_out = tables
    positions = jnp.arange(SEQ, dtype=jnp.int32)
    segment, req_begin, req_owner = request_info(lengths, adapter_ids, positions)
    adapter_onehot = (req_owner[:, None] == jnp.arange(ADAPTERS, dtype=jnp.int32)).astype(jnp.bfloat16)
    onehot_float = adapter_onehot.astype(jnp.float32)
    every_term = jnp.dot(input_rows, down_adapter.reshape(ADAPTERS * 3 * ADAPTER_RANK, MODEL_WIDTH).T, preferred_element_type=jnp.float32)
    every_term = every_term.reshape(SEQ, ADAPTERS, 3 * ADAPTER_RANK)
    adapter_middle = lax.optimization_barrier(jnp.sum(every_term * onehot_float[:, :, None], axis=1)).astype(jnp.bfloat16)
    offsets = (positions - req_begin).astype(jnp.float32)
    query_total = jnp.dot(input_rows, query_weight, preferred_element_type=jnp.float32) + ADAPTER_SCALE * widen_rows(adapter_middle[:, 0:ADAPTER_RANK], adapter_onehot, up_query_adapter)
    key_total = jnp.dot(input_rows, key_weight, preferred_element_type=jnp.float32) + ADAPTER_SCALE * widen_rows(adapter_middle[:, ADAPTER_RANK:2 * ADAPTER_RANK], adapter_onehot, up_key_adapter)
    value_total = jnp.dot(input_rows, value_weight, preferred_element_type=jnp.float32) + ADAPTER_SCALE * widen_rows(adapter_middle[:, 2 * ADAPTER_RANK:3 * ADAPTER_RANK], adapter_onehot, up_value_adapter)
    query = rotate(query_total.reshape(SEQ, QH, HD), offsets).astype(jnp.bfloat16)
    key = rotate(key_total.reshape(SEQ, KVH, HD), offsets).astype(jnp.bfloat16)
    value = value_total.reshape(SEQ, KVH, HD).astype(jnp.bfloat16)
    query_groups = query.reshape(SEQ, KVH, QH // KVH, HD).astype(jnp.float32)
    scores = jnp.einsum('tkjd,skd->tkjs', query_groups, key.astype(jnp.float32)) / math.sqrt(HD)
    allowed = (segment[:, None] == segment[None, :]) & (positions[None, :] <= positions[:, None])
    allowed = allowed[:, None, None, :]
    scores = jnp.where(allowed, scores, MASKED_SCORE)
    row_top = lax.optimization_barrier(jnp.max(scores, axis=-1, keepdims=True))
    weights = jnp.where(allowed, jnp.exp(scores - row_top), 0.0)
    weight_sum = lax.optimization_barrier(jnp.sum(weights, axis=-1))
    rounded = lax.optimization_barrier(weights.astype(jnp.bfloat16)).astype(jnp.float32)
    attended = jnp.einsum('tkjs,skd->tkjd', rounded, value.astype(jnp.float32)) / weight_sum[..., None]
    attended = attended.reshape(SEQ, QH * HD).astype(jnp.bfloat16)
    mid_terms = jnp.dot(attended, downo_ad.reshape(ADAPTERS * ADAPTER_RANK, QH * HD).T, preferred_element_type=jnp.float32)
    output_middle = lax.optimization_barrier(jnp.sum(mid_terms.reshape(SEQ, ADAPTERS, ADAPTER_RANK) * onehot_float[:, :, None], axis=1)).astype(jnp.bfloat16)
    head_cols = QH * HD // N_GRP
    base_product = jnp.zeros((SEQ, MODEL_WIDTH), jnp.float32)
    for shard in range(N_GRP):
        partial_term = jnp.dot(attended[:, shard * head_cols:(shard + 1) * head_cols], w_out[shard * head_cols:(shard + 1) * head_cols], preferred_element_type=jnp.float32)
        base_product = base_product + lax.optimization_barrier(partial_term.astype(jnp.bfloat16)).astype(jnp.float32)
    adapter_delta = widen_rows(output_middle, adapter_onehot, up_output_adapter)
    return (base_product + ADAPTER_SCALE * adapter_delta).astype(jnp.bfloat16)

def reference(tokens, req_lengths, req_adapter, adapter_slot, query_weight, key_weight, value_weight, w_out, down_qkv, up_query, up_kv, down_out, up_out):
    up_key_value_adapter = up_kv[adapter_slot]
    tables = (down_qkv[adapter_slot], up_query[adapter_slot], up_key_value_adapter[:, 0], up_key_value_adapter[:, 1], down_out[adapter_slot], up_out[adapter_slot], query_weight, key_weight, value_weight, w_out)

    def run_group(group_data):
        return one_group(group_data[0], group_data[1], group_data[2], tables)
    return lax.map(run_group, (tokens, req_lengths, req_adapter))
```

```python
import functools
import math

import jax
import jax.numpy as jnp
import numpy as np
from jax import lax
from jax.experimental import pallas as pl
from jax.experimental.pallas import tpu as pltpu
from jax.sharding import PartitionSpec as P

D = 4096
HD = 128
RK = 16
REQS = 8
ROPE_BASE = 500000.0
MESH = pl.DeviceIdType.MESH
F32 = jnp.float32
BF16 = jnp.bfloat16
NEG = -1e30

QC = 512
KVC = 128
HR = 32
KCH = 1024
NCH = D // KCH
NJ = 2 * NCH
LEAD = 3


class Place:
    def __init__(self):
        self.g = lax.axis_index("grp")
        self.c = lax.axis_index("ctx")
        self.y = self.g // 2
        self.xl = self.g % 2
        self.z = self.c // 4
        self.xh = (self.c // 2) % 2
        self.co = self.c % 2
        self.xh2 = (self.xh + self.co) % 2

    def group(self, dy, flip):
        return ((self.y + dy) % 4) * 2 + (self.xl + flip) % 2

    def peer(self, dy, flip):
        ctx = self.z * 4 + self.xh2 * 2 + self.co if flip else self.c
        return (self.group(dy, flip), ctx)

    def level(self, z):
        return (self.g, z * 4 + self.xh * 2 + self.co)

    def quarter(self, b):
        xh = jnp.where((b % 2) == self.xl, self.xh, self.xh2)
        return xh * 2 + self.co


PEERS = [(dy, flip) for dy in range(4) for flip in range(2)][1:]


def rcopy(src, dst, ssem, rsem, device):
    return pltpu.make_async_remote_copy(
        src_ref=src, dst_ref=dst, send_sem=ssem, recv_sem=rsem, device_id=device, device_id_type=MESH
    )


def greet(devices):
    barrier = pltpu.get_barrier_semaphore()
    for device in devices:
        pl.semaphore_signal(barrier, inc=1, device_id=device, device_id_type=MESH)
    pl.semaphore_wait(barrier, len(devices))


def row_slots(place, half, lens, adap, aslot):
    lane = lax.broadcasted_iota(jnp.int32, (8, 256), 1)
    out = jnp.zeros((8, 256), jnp.int32)
    for b in range(8):
        pos = 64 * (place.z * 4 + place.quarter(b)) + HR * half + lane - b * HR
        mine = (lane >= b * HR) & (lane < (b + 1) * HR)
        end = jnp.int32(0)
        for r in range(REQS):
            begin = end
            end = begin + lens[b, r]
            hit = mine & (pos >= begin) & (pos < end)
            out = jnp.where(hit, aslot[adap[b, r]], out)
    return out


def front_kernel(
    lens, adap, aslot, tok, wq, wk, wv, dn, uq, ukv, freq,
    q_out, kv_out,
    xall, w, acc, accm, uq_all, uk_all, uv_all, midsend, mid_all, qbuf, kvbuf, cosb, sinb,
    lsem, tsem_s, tsem_r, ss, rr, ms, mr, zs, zr, gs, gr, osem,
):
    pc = Place()
    z = pc.z
    partner = pc.peer(0, 1)
    up = pc.peer(1, 0)
    down = pc.peer(3, 0)
    mate = (pc.g, z * 4 + pc.xh * 2 + 1 - pc.co)
    across = (pc.g, z * 4 + (1 - pc.xh) * 2 + pc.co)

    loads = [
        pltpu.make_async_copy(wq, w.at[:, 0:QC], lsem.at[0]),
        pltpu.make_async_copy(wk, w.at[:, QC : QC + KVC], lsem.at[1]),
        pltpu.make_async_copy(wv, w.at[:, QC + KVC : QC + 2 * KVC], lsem.at[2]),
        pltpu.make_async_copy(tok.at[0:HR, :], xall.at[0, pc.g], lsem.at[3]),
        pltpu.make_async_copy(tok.at[HR : 2 * HR, :], xall.at[1, pc.g], lsem.at[4]),
    ]
    for load in loads:
        load.start()

    greet(
        [pc.peer(*p) for p in PEERS]
        + [pc.level((z + d) % 8) for d in range(1, 8)]
        + [mate, across]
    )

    def part(J):
        return J // NCH, pl.ds(pl.multiple_of((J % NCH) * KCH, KCH), KCH)

    def block(J, group):
        h, cols = part(J)
        return xall.at[h, group, :, cols]

    def own_copies(J):
        h, cols = part(J)
        src = tok.at[pl.ds(pl.multiple_of(h * HR, HR), HR), cols]
        dst = block(J, pc.g)
        return (
            rcopy(src, dst, ss.at[J, 0], rr.at[J, 2], up),
            rcopy(src, dst, ss.at[J, 1], rr.at[J, 3], down),
            rcopy(src, dst, ss.at[J, 2], rr.at[J, 1], partner),
        )

    def forward(J, slot, group, ssem, rslot, device):
        ref = block(J, group)
        return rcopy(ref, ref, ss.at[J, ssem], rr.at[J, rslot], device)

    g_dn, g_up, g_far = pc.group(3, 0), pc.group(1, 0), pc.group(2, 0)

    def waiting(J, slot, group):
        ref = block(J, group)
        return rcopy(ref, ref, ss.at[J, 0], rr.at[J, slot], partner)

    def own(J):
        for copy in own_copies(J):
            copy.start()

    def stage_a(J):
        waiting(J, 2, g_dn).wait_recv()
        forward(J, 2, g_dn, 3, 4, partner).start()

        @pl.when(J % 2 == 0)
        def _():
            forward(J, 2, g_dn, 6, 6, up).start()

        waiting(J, 3, g_up).wait_recv()
        forward(J, 3, g_up, 4, 5, partner).start()

        @pl.when(J % 2 == 1)
        def _():
            forward(J, 3, g_up, 6, 6, down).start()

    def stage_b(J):
        waiting(J, 6, g_far).wait_recv()
        forward(J, 6, g_far, 5, 7, partner).start()

    def stage_c(J):
        for slot, dy in ((1, 0), (4, 3), (5, 1), (7, 2)):
            waiting(J, slot, pc.group(dy, 1)).wait_recv()
        h, cols = part(J)
        x = xall[h, :, :, cols].reshape(8 * HR, KCH)

        @pl.when(J % NCH == 0)
        def _():
            acc[h] = jnp.zeros(acc.shape[1:], F32)
            accm[h] = jnp.zeros(accm.shape[1:], F32)

        rows = pl.ds(pl.multiple_of((J % NCH) * KCH, KCH), KCH)
        accm[h] += lax.dot_general(
            dn[:, cols], x, (((1,), (1,)), ((), ())), preferred_element_type=F32
        )
        acc[h] += jnp.dot(x, w[rows, :], preferred_element_type=F32)

    def step(t, carry=None):
        @pl.when(t + LEAD < NJ)
        def _():
            own(t + LEAD)

        @pl.when(t < NJ)
        def _():
            stage_a(t)

        @pl.when((t >= 1) & (t < NJ + 1))
        def _():
            stage_b(t - 1)

        @pl.when(t >= 2)
        def _():
            stage_c(t - 2)

        return carry

    for J in range(LEAD):
        own(J)

    def table_copies(k, dy, flip):
        device = pc.peer(dy, flip)
        i = pc.group(dy, flip)
        qcols = pl.ds(pl.multiple_of(i * QC, QC), QC)
        kcols = pl.ds(pl.multiple_of(i * KVC, KVC), KVC)
        return (
            rcopy(uq.at[:, qcols], uq_all.at[pc.g], tsem_s.at[k, 0], tsem_r.at[k, 0], device),
            rcopy(ukv.at[0, :, kcols], uk_all.at[pc.g], tsem_s.at[k, 1], tsem_r.at[k, 1], device),
            rcopy(ukv.at[1, :, kcols], uv_all.at[pc.g], tsem_s.at[k, 2], tsem_r.at[k, 2], device),
        )

    for k, (dy, flip) in enumerate(PEERS):
        for copy in table_copies(k, dy, flip):
            copy.start()
    qcols = pl.ds(pl.multiple_of(pc.g * QC, QC), QC)
    kcols = pl.ds(pl.multiple_of(pc.g * KVC, KVC), KVC)
    uq_all[pc.g] = uq[:, qcols]
    uk_all[pc.g] = ukv[0, :, kcols]
    uv_all[pc.g] = ukv[1, :, kcols]

    sub = lax.broadcasted_iota(jnp.int32, (HR, HD), 0)
    low = lax.broadcasted_iota(jnp.int32, (HR, HD), 1) < HD // 2
    for half in range(2):
        for b in range(8):
            pos = 64 * (z * 4 + pc.quarter(b)) + HR * half + sub
            begin = jnp.zeros((HR, HD), jnp.int32)
            end = jnp.int32(0)
            for r in range(REQS):
                length = lens[b, r]
                end = end + length
                begin = begin + jnp.where(pos >= end, length, 0)
            angle = (pos - begin).astype(F32) * freq[...]
            rows = pl.ds(half * 256 + b * HR, HR)
            cosb[rows, :] = jnp.cos(angle)
            sine = jnp.sin(angle)
            sinb[rows, :] = jnp.where(low, -sine, sine)

    for load in loads:
        load.wait()

    def mid_copies(half):
        return [
            rcopy(midsend.at[half], mid_all.at[half, pc.g], ms.at[half, k], mr.at[half, k], pc.peer(*p))
            for k, p in enumerate(PEERS)
        ]

    def finish_mid(half):
        keep = (row_slots(pc, half, lens, adap, aslot)[0:1, :] == pc.g).astype(F32)
        mid = (accm[half] * keep).astype(BF16).reshape(3, RK, 256)
        midsend[half] = mid
        mid_all[half, pc.g] = mid
        for copy in mid_copies(half):
            copy.start()

    def z_copies(half, d):
        zd = (z + d) % 8
        quarter = pc.quarter(zd)
        return (
            rcopy(kvbuf.at[half, zd], kv_out.at[z, quarter, half], zs.at[half, d, 1], zr.at[half, d, 1], pc.level(zd)),
            rcopy(qbuf.at[half, zd], q_out.at[z, half], zs.at[half, d, 0], zr.at[half, d, 0], pc.level(zd)),
        )

    def own_out(half):
        return (
            pltpu.make_async_copy(kvbuf.at[half, z], kv_out.at[z, pc.quarter(z), half], osem.at[half, 1]),
            pltpu.make_async_copy(qbuf.at[half, z], q_out.at[z, half], osem.at[half, 0]),
        )

    def finish_rows(half):
        for copy in mid_copies(half):
            copy.wait_recv()
        rows = pl.ds(half * 256, 256)
        cosv, sinv = cosb[rows, :], sinb[rows, :]

        def widen(which, table, base):
            mid = mid_all[half, :, which].reshape(8 * RK, 256)
            n = table.shape[2]
            delta = lax.dot_general(
                mid, table[...].reshape(8 * RK, n), (((0,), (0,)), ((), ())), preferred_element_type=F32
            )
            return base + 2.0 * delta

        def rope(v):
            return v * cosv + pltpu.roll(v, HD // 2, 1) * sinv

        query = widen(0, uq_all, acc[half, :, 0:QC])
        for j in range(4):
            qbuf[half, :, :, j * HD : (j + 1) * HD] = (
                rope(query[:, j * HD : (j + 1) * HD]).astype(BF16).reshape(8, HR, HD)
            )
        key = rope(widen(1, uk_all, acc[half, :, QC : QC + KVC]))
        kvbuf[half, :, :, 0:HD] = key.astype(BF16).reshape(8, HR, HD)
        value = widen(2, uv_all, acc[half, :, QC + KVC : QC + 2 * KVC])
        kvbuf[half, :, :, HD : 2 * HD] = value.astype(BF16).reshape(8, HR, HD)
        for d in (4, 3, 5, 2, 6, 1, 7):
            for copy in z_copies(half, d):
                copy.start()
        for copy in own_out(half):
            copy.start()

    q_own = pc.quarter(z)
    q_across = (1 - q_own // 2) * 2 + pc.co
    xh_mate = jnp.where((z % 2) == pc.xl, pc.xh, (pc.xh + 1 - pc.co) % 2)
    q_mate = xh_mate * 2 + 1 - pc.co
    q_mate_across = (1 - xh_mate) * 2 + 1 - pc.co

    def column(quarter, half):
        return kv_out.at[:, quarter, half]

    def kv_copy(quarter, half, k, device):
        ref = column(quarter, half)
        return rcopy(ref, ref, gs.at[half, k], gr.at[half, k], device)

    def spread_own(half):
        for copy in own_out(half):
            copy.wait()
        for d in range(1, 8):
            z_copies(half, d)[0].wait_recv()
        kv_copy(q_own, half, 1, across).start()
        kv_copy(q_own, half, 0, mate).start()

    def spread_across(half):
        kv_copy(q_across, half, 1, across).wait_recv()
        kv_copy(q_across, half, 2, mate).start()

    lax.fori_loop(0, NCH + 2, step, None)
    for k, (dy, flip) in enumerate(PEERS):
        for copy in table_copies(k, dy, flip):
            copy.wait_recv()
    finish_mid(0)
    lax.fori_loop(NCH + 2, NJ, step, None)
    finish_rows(0)
    lax.fori_loop(NJ, NJ + 2, step, None)
    finish_mid(1)
    spread_own(0)
    finish_rows(1)
    spread_across(0)
    spread_own(1)
    spread_across(1)

    for half in range(2):
        kv_copy(q_mate, half, 0, mate).wait_recv()
        kv_copy(q_mate_across, half, 2, mate).wait_recv()
        for d in range(1, 8):
            kv, q = z_copies(half, d)
            q.wait_recv()
            kv.wait_send()
            q.wait_send()
        kv_copy(q_own, half, 1, across).wait_send()
        kv_copy(q_own, half, 0, mate).wait_send()
        kv_copy(q_across, half, 2, mate).wait_send()
        for copy in mid_copies(half):
            copy.wait_send()
    for k, (dy, flip) in enumerate(PEERS):
        for copy in table_copies(k, dy, flip):
            copy.wait_send()

    def drain(J, carry):
        for copy in own_copies(J):
            copy.wait_send()
        for k in range(3, 7):
            forward(J, 0, pc.g, k, 0, partner).wait_send()
        return carry

    lax.fori_loop(0, NJ, drain, None)


def front(lens, adap, aslot, tok, wq, wk, wv, dn, uq, ukv, freq):
    any_ = pl.BlockSpec(memory_space=pl.ANY)
    vmem = pl.BlockSpec(memory_space=pltpu.VMEM)
    smem = pl.BlockSpec(memory_space=pltpu.SMEM)
    dma = pltpu.SemaphoreType.DMA
    return pl.pallas_call(
        front_kernel,
        name="front",
        out_shape=(
            jax.ShapeDtypeStruct((8, 2, HR, QC), BF16),
            jax.ShapeDtypeStruct((8, 4, 2, HR, 2 * HD), BF16),
        ),
        in_specs=[smem] * 3 + [any_] * 4 + [vmem] * 4,
        out_specs=(any_, any_),
        scratch_shapes=[
            pltpu.VMEM((2, 8, HR, D), BF16),
            pltpu.VMEM((D, QC + 2 * KVC), BF16),
            pltpu.VMEM((2, 256, QC + 2 * KVC), F32),
            pltpu.VMEM((2, 3 * RK, 256), F32),
            pltpu.VMEM((8, RK, QC), BF16),
            pltpu.VMEM((8, RK, KVC), BF16),
            pltpu.VMEM((8, RK, KVC), BF16),
            pltpu.VMEM((2, 3, RK, 256), BF16),
            pltpu.VMEM((2, 8, 3, RK, 256), BF16),
            pltpu.VMEM((2, 8, HR, QC), BF16),
            pltpu.VMEM((2, 8, HR, 2 * HD), BF16),
            pltpu.VMEM((512, HD), F32),
            pltpu.VMEM((512, HD), F32),
            dma((5,)),
            dma((7, 3)),
            dma((7, 3)),
            dma((NJ, 7)),
            dma((NJ, 8)),
            dma((2, 7)),
            dma((2, 7)),
            dma((2, 8, 2)),
            dma((2, 8, 2)),
            dma((2, 3)),
            dma((2, 3)),
            dma((2, 2)),
        ],
        compiler_params=pltpu.CompilerParams(
            collective_id=0, has_side_effects=True, vmem_limit_bytes=60 << 20
        ),
    )(lens, adap, aslot, tok, wq, wk, wv, dn, uq, ukv, freq)


CK = 256


def attend_kernel(lens, q_ref, kv_ref, o_ref):
    pc = Place()
    z = pc.z
    zs = pl.program_id(0)
    quarter = pc.quarter(z)
    first = 64 * (zs * 4 + quarter)
    row = lax.broadcasted_iota(jnp.int32, (256, CK), 0) % 64
    col = lax.broadcasted_iota(jnp.int32, (256, CK), 1)
    pos = first + row
    begin = jnp.zeros((256, CK), jnp.int32)
    end = jnp.int32(0)
    head = jnp.int32(0)
    for r in range(REQS):
        length = lens[z, r]
        end = end + length
        begin = begin + jnp.where(pos >= end, length, 0)
        head = head + jnp.where(first >= end, length, 0)
    q = q_ref[...].reshape(64, QC)
    q = jnp.concatenate([q[:, j * HD : (j + 1) * HD] for j in range(4)], axis=0)
    scale = 1.0 / math.sqrt(HD)

    def chunk(j, state):
        top, total, accum = state
        keys = kv_ref[j, :, 0:HD]
        values = kv_ref[j, :, HD : 2 * HD]
        s = lax.dot_general(q, keys, (((1,), (1,)), ((), ())), preferred_element_type=F32) * scale
        at = j * CK + col
        kept = (at >= begin) & (at <= pos)
        s = jnp.where(kept, s, NEG)
        new = jnp.maximum(top, jnp.max(s, axis=1, keepdims=True))
        p = jnp.where(kept, jnp.exp(s - new), 0.0)
        fade = jnp.exp(top - new)
        total = total * fade + jnp.sum(p, axis=1, keepdims=True)
        accum = accum * fade + jnp.dot(p.astype(BF16), values, preferred_element_type=F32)
        return new, total, accum

    state = (
        jnp.full((256, 1), NEG, F32),
        jnp.zeros((256, 1), F32),
        jnp.zeros((256, HD), F32),
    )
    top, total, accum = lax.fori_loop(head // CK, zs + 1, chunk, state)
    out = (accum / total).astype(BF16)
    for j in range(4):
        o_ref[0, :, :, j * HD : (j + 1) * HD] = out[j * 64 : (j + 1) * 64].reshape(2, HR, HD)


def attend(lens, q, kv):
    return pl.pallas_call(
        attend_kernel,
        name="attend",
        grid=(8,),
        out_shape=jax.ShapeDtypeStruct((8, 2, HR, QC), BF16),
        in_specs=[
            pl.BlockSpec(memory_space=pltpu.SMEM),
            pl.BlockSpec((1, 2, HR, QC), lambda i: (i, 0, 0, 0)),
            pl.BlockSpec((8, 256, 2 * HD), lambda i: (0, 0, 0)),
        ],
        out_specs=pl.BlockSpec((1, 2, HR, QC), lambda i: (i, 0, 0, 0)),
        compiler_params=pltpu.CompilerParams(vmem_limit_bytes=40 << 20),
    )(lens, q, kv.reshape(8, 256, 2 * HD))


NC = 512
NN = D // NC
NT = 2 * NN


def back_kernel(
    lens, adap, aslot, att, w_out, do, uo,
    out,
    w, att_all, do_all, omsend, om_recv, om, pbuf, xrecv, sbuf, far, tup, tdn, rup, rdn,
    lsem, ds_s, ds_r, zs, zr, os_, or_, xs, xr, ys, yr, osem,
):
    pc = Place()
    z = pc.z
    partner = pc.peer(0, 1)
    up = pc.peer(1, 0)
    down = pc.peer(3, 0)

    load = pltpu.make_async_copy(w_out, w, lsem.at[0])
    load.start()
    own_att = [pltpu.make_async_copy(att.at[z, h], att_all.at[h, z], osem.at[h]) for h in range(2)]
    for copy in own_att:
        copy.start()
    own_do = pltpu.make_async_copy(
        do.at[:, pl.ds(pl.multiple_of(pc.g * QC, QC), QC)], do_all.at[pc.g], lsem.at[1]
    )
    own_do.start()

    greet([pc.peer(*p) for p in PEERS] + [pc.level((z + d) % 8) for d in range(1, 8)])

    def z_copy(half, d):
        zd = (z + d) % 8
        return rcopy(att.at[zd, half], att_all.at[half, z], zs.at[half, d], zr.at[half, d], pc.level(zd))

    for half in range(2):
        for d in (4, 3, 5, 2, 6, 1, 7):
            z_copy(half, d).start()

    def do_copy(k, dy, flip):
        i = pc.group(dy, flip)
        cols = pl.ds(pl.multiple_of(i * QC, QC), QC)
        return rcopy(do.at[:, cols], do_all.at[pc.g], ds_s.at[k], ds_r.at[k], pc.peer(dy, flip))

    for k, p in enumerate(PEERS):
        do_copy(k, *p).start()
    load.wait()
    own_do.wait()
    for k, p in enumerate(PEERS):
        do_copy(k, *p).wait_recv()

    def om_copy(half, k, dy, flip):
        i = pc.group(dy, flip)
        return rcopy(
            omsend.at[half, i], om_recv.at[half, pc.g], os_.at[half, k], or_.at[half, k], pc.peer(dy, flip)
        )

    def mid_send(half):
        own_att[half].wait()
        for d in range(1, 8):
            z_copy(half, d).wait_recv()
        rows = att_all[half].reshape(256, QC)
        mid = lax.dot_general(
            do_all[...].reshape(8 * RK, QC), rows, (((1,), (1,)), ((), ())), preferred_element_type=F32
        ).reshape(8, RK, 256)
        omsend[half] = mid
        for k, p in enumerate(PEERS):
            om_copy(half, k, *p).start()
        om_recv[half, pc.g] = omsend[half, pc.g]

    def mid_done(half):
        for k, p in enumerate(PEERS):
            om_copy(half, k, *p).wait_recv()
        keep = (row_slots(pc, half, lens, adap, aslot)[0:1, :] == pc.g).astype(F32)
        om[half] = (jnp.sum(om_recv[half], axis=0) * keep).astype(BF16)

    y_far, y_up, y_dn = (pc.y + 2) % 4, (pc.y + 1) % 4, (pc.y + 3) % 4

    def x_copy(J):
        return rcopy(pbuf.at[J, :, 1 - pc.xl], xrecv.at[J], xs.at[J], xr.at[J], partner)

    def far_copy(J, odd):
        device = down if odd else up
        return rcopy(sbuf.at[J, y_far], far.at[J], ys.at[J, 0], yr.at[J, 0], device)

    def up_copy(J):
        return rcopy(tup.at[J], rup.at[J], ys.at[J, 1], yr.at[J, 1], up)

    def dn_copy(J):
        return rcopy(tdn.at[J], rdn.at[J], ys.at[J, 2], yr.at[J, 2], down)

    def stage_p(J):
        half = J // NN
        cols = pl.ds(pl.multiple_of((J % NN) * NC, NC), NC)
        rows = att_all[half].reshape(256, QC)
        total = jnp.dot(rows, w[:, cols], preferred_element_type=F32) + 2.0 * lax.dot_general(
            om[half], uo[:, cols], (((0,), (0,)), ((), ())), preferred_element_type=F32
        )
        pbuf[J] = total.astype(BF16).reshape(4, 2, HR, NC)
        x_copy(J).start()

    def stage_s(J, odd):
        x_copy(J).wait_recv()
        total = pbuf[J, :, pc.xl].astype(F32) + xrecv[J].astype(F32)
        sbuf[J] = total.astype(BF16)
        far_copy(J, odd).start()
        if odd:
            tup[J] = sbuf[J, y_up]
            up_copy(J).start()
        else:
            tdn[J] = sbuf[J, y_dn]
            dn_copy(J).start()

    def stage_t(J, odd):
        far_copy(J, odd).wait_recv()
        if odd:
            tdn[J] = (sbuf[J, y_dn].astype(F32) + far[J].astype(F32)).astype(BF16)
            dn_copy(J).start()
        else:
            tup[J] = (sbuf[J, y_up].astype(F32) + far[J].astype(F32)).astype(BF16)
            up_copy(J).start()

    def stage_f(J):
        up_copy(J).wait_recv()
        dn_copy(J).wait_recv()
        half = J // NN
        cols = pl.ds(pl.multiple_of((J % NN) * NC, NC), NC)
        total = sbuf[J, pc.y].astype(F32) + rup[J].astype(F32) + rdn[J].astype(F32)
        out[pl.ds(pl.multiple_of(half * HR, HR), HR), cols] = total.astype(BF16)

    def step(t, carry=None):
        @pl.when(t < NT // 2)
        def _():
            stage_p(2 * t)
            stage_p(2 * t + 1)

        @pl.when((t >= 1) & (t < NT // 2 + 1))
        def _():
            stage_s(2 * t - 2, False)
            stage_s(2 * t - 1, True)

        @pl.when((t >= 2) & (t < NT // 2 + 2))
        def _():
            stage_t(2 * t - 4, False)
            stage_t(2 * t - 3, True)

        @pl.when(t >= 3)
        def _():
            stage_f(2 * t - 6)
            stage_f(2 * t - 5)

        return carry

    mid_send(0)
    mid_done(0)
    lax.fori_loop(0, 2, step, None)
    mid_send(1)
    lax.fori_loop(2, NN // 2, step, None)
    mid_done(1)
    lax.fori_loop(NN // 2, NT // 2 + 3, step, None)

    for half in range(2):
        for d in range(1, 8):
            z_copy(half, d).wait_send()
        for k, p in enumerate(PEERS):
            om_copy(half, k, *p).wait_send()
    for k, p in enumerate(PEERS):
        do_copy(k, *p).wait_send()

    def drain(J, carry):
        x_copy(J).wait_send()
        far_copy(J, False).wait_send()
        up_copy(J).wait_send()
        dn_copy(J).wait_send()
        return carry

    lax.fori_loop(0, NT, drain, None)


def back(lens, adap, aslot, att, w_out, do, uo):
    any_ = pl.BlockSpec(memory_space=pl.ANY)
    vmem = pl.BlockSpec(memory_space=pltpu.VMEM)
    smem = pl.BlockSpec(memory_space=pltpu.SMEM)
    dma = pltpu.SemaphoreType.DMA
    return pl.pallas_call(
        back_kernel,
        name="back",
        out_shape=jax.ShapeDtypeStruct((64, D), BF16),
        in_specs=[smem] * 3 + [any_] * 3 + [vmem],
        out_specs=vmem,
        scratch_shapes=[
            pltpu.VMEM((QC, D), BF16),
            pltpu.VMEM((2, 8, HR, QC), BF16),
            pltpu.VMEM((8, RK, QC), BF16),
            pltpu.VMEM((2, 8, RK, 256), F32),
            pltpu.VMEM((2, 8, RK, 256), F32),
            pltpu.VMEM((2, RK, 256), BF16),
            pltpu.VMEM((NT, 4, 2, HR, NC), BF16),
            pltpu.VMEM((NT, 4, HR, NC), BF16),
            pltpu.VMEM((NT, 4, HR, NC), BF16),
            pltpu.VMEM((NT, HR, NC), BF16),
            pltpu.VMEM((NT, HR, NC), BF16),
            pltpu.VMEM((NT, HR, NC), BF16),
            pltpu.VMEM((NT, HR, NC), BF16),
            pltpu.VMEM((NT, HR, NC), BF16),
            dma((2,)),
            dma((7,)),
            dma((7,)),
            dma((2, 8)),
            dma((2, 8)),
            dma((2, 7)),
            dma((2, 7)),
            dma((NT,)),
            dma((NT,)),
            dma((NT, 3)),
            dma((NT, 3)),
            dma((2,)),
        ],
        compiler_params=pltpu.CompilerParams(
            collective_id=1, has_side_effects=True, vmem_limit_bytes=60 << 20
        ),
    )(lens, adap, aslot, att, w_out, do, uo)


def body(
    tokens, req_lengths, req_adapter, adapter_slot, query_weight, key_weight, value_weight, w_out,
    down_qkv, up_query, up_kv, down_out, up_out,
):
    half = np.arange(HD) % (HD // 2)
    freq = jnp.asarray(np.exp(half * (-2.0 * math.log(ROPE_BASE) / HD)).astype(np.float32)[None, :])
    q, kv = front(
        req_lengths, req_adapter, adapter_slot, tokens[0], query_weight, key_weight, value_weight,
        down_qkv[0], up_query[0], up_kv[0], freq,
    )
    att = attend(req_lengths, q, kv)
    out = back(req_lengths, req_adapter, adapter_slot, att, w_out, down_out[0], up_out[0])
    return out[None]


def solution(mesh):
    placed = (
        P("grp", "ctx", None),
        P(),
        P(),
        P(),
        P(None, "grp"),
        P(None, "grp"),
        P(None, "grp"),
        P("grp", None),
        P("grp", None, None),
        P("grp", None, None),
        P("grp", None, None, None),
        P("grp", None, None),
        P("grp", None, None),
    )
    return jax.shard_map(
        body, mesh=mesh, in_specs=placed, out_specs=P("grp", "ctx", None), check_vma=False
    )
```

```python
import functools
import math

import jax
import jax.numpy as jnp
import numpy as np
from jax import lax
from jax.experimental import pallas as pl
from jax.experimental.pallas import tpu as pltpu
from jax.sharding import PartitionSpec as P

D = 4096
HD = 128
RK = 16
REQS = 8
ROPE_BASE = 500000.0
MESH = pl.DeviceIdType.MESH
F32 = jnp.float32
BF16 = jnp.bfloat16
NEG = -1e30

QC = 512
KVC = 128
H = 4
HR = 64 // H
NR = 8 * HR
NCH = 4
KCH = D // NCH
NJ = H * NCH
LEAD = 5
LAG_B, LAG_C, LAG_ROWS, LAG_OWN, LAG_ACROSS = 2, 5, 7, 11, 13
BR = 32
CK = 384
NK = -(-(1088 + BR - 1) // CK)
NC = 512
NN = D // NC
NT = 2 * NN


class Place:
    def __init__(self):
        self.g = lax.axis_index("grp")
        self.c = lax.axis_index("ctx")
        self.y = self.g // 2
        self.xl = self.g % 2
        self.z = self.c // 4
        self.xh = (self.c // 2) % 2
        self.co = self.c % 2
        self.xh2 = (self.xh + self.co) % 2

    def group(self, dy, flip):
        return ((self.y + dy) % 4) * 2 + (self.xl + flip) % 2

    def peer(self, dy, flip):
        ctx = self.z * 4 + self.xh2 * 2 + self.co if flip else self.c
        return (self.group(dy, flip), ctx)

    def level(self, z):
        return (self.g, z * 4 + self.xh * 2 + self.co)

    def quarter(self, b):
        xh = jnp.where((b % 2) == self.xl, self.xh, self.xh2)
        return xh * 2 + self.co


PEERS = [(dy, flip) for dy in range(4) for flip in range(2)][1:]


def rcopy(src, dst, ssem, rsem, device):
    return pltpu.make_async_remote_copy(
        src_ref=src, dst_ref=dst, send_sem=ssem, recv_sem=rsem, device_id=device, device_id_type=MESH
    )


def greet(devices):
    barrier = pltpu.get_barrier_semaphore()
    for device in devices:
        pl.semaphore_signal(barrier, inc=1, device_id=device, device_id_type=MESH)
    pl.semaphore_wait(barrier, len(devices))


def row_slots(place, groups, rows, offset, lens, adap, aslot):
    lane = lax.broadcasted_iota(jnp.int32, (8, len(groups) * rows), 1)
    out = jnp.zeros(lane.shape, jnp.int32)
    for i, b in enumerate(groups):
        pos = 64 * (place.z * 4 + place.quarter(b)) + offset + lane - i * rows
        mine = (lane >= i * rows) & (lane < (i + 1) * rows)
        end = jnp.int32(0)
        for r in range(REQS):
            begin = end
            end = begin + lens[b, r]
            hit = mine & (pos >= begin) & (pos < end)
            out = jnp.where(hit, aslot[adap[b, r]], out)
    return out[0:1, :]


def layer_kernel(
    lens, adap, aslot, tok, wq, wk, wv, w_out, dn_hbm, uq, ukv, do, uo_hbm, freq,
    out,
    xall, w, wo, dn, uo, acc, accm, uq_all, uk_all, uv_all, do_all, midsend, mid_all, qbuf, kvbuf,
    cosb, sinb, q_all, kv_all, att_buf, att_all, omsend, om_recv, om, pbuf, xrecv, sbuf, far, tup, tdn, rup, rdn,
    lsem, ts, tr, ss, rr, ms, mr, zs_s, zs_r, gs, gr, as_, ar, os_, or_, xs, xr, ys, yr,
):
    pc = Place()
    z = pc.z
    partner = pc.peer(0, 1)
    up = pc.peer(1, 0)
    down = pc.peer(3, 0)
    mate = (pc.g, z * 4 + pc.xh * 2 + 1 - pc.co)
    across = (pc.g, z * 4 + (1 - pc.xh) * 2 + pc.co)
    qcols = pl.ds(pl.multiple_of(pc.g * QC, QC), QC)
    kcols = pl.ds(pl.multiple_of(pc.g * KVC, KVC), KVC)

    local = [
        (wq, w.at[:, 0:QC]),
        (wk, w.at[:, QC : QC + KVC]),
        (wv, w.at[:, QC + KVC : QC + 2 * KVC]),
        (dn_hbm, dn),
        (uq.at[:, qcols], uq_all.at[pc.g]),
        (ukv.at[0, :, kcols], uk_all.at[pc.g]),
        (ukv.at[1, :, kcols], uv_all.at[pc.g]),
        (do.at[:, qcols], do_all.at[pc.g]),
    ] + [(tok.at[h * HR : (h + 1) * HR, :], xall.at[h, pc.g]) for h in range(H)] + [
        (uo_hbm, uo.at[pc.xl]),
        (w_out, wo),
    ]
    loads = [pltpu.make_async_copy(src, dst, lsem.at[i]) for i, (src, dst) in enumerate(local)]
    for load in loads:
        load.start()

    greet(
        [pc.peer(*p) for p in PEERS]
        + [pc.level((z + d) % 8) for d in range(1, 8)]
        + [mate, across]
    )

    def part(J):
        return J // NCH, pl.ds(pl.multiple_of((J % NCH) * KCH, KCH), KCH)

    def block(J, group):
        h, cols = part(J)
        return xall.at[h, group, :, cols]

    def own_copies(J):
        h, cols = part(J)
        src = tok.at[pl.ds(pl.multiple_of(h * HR, HR), HR), cols]
        dst = block(J, pc.g)
        return (
            rcopy(src, dst, ss.at[J, 0], rr.at[J, 2], up),
            rcopy(src, dst, ss.at[J, 1], rr.at[J, 3], down),
            rcopy(src, dst, ss.at[J, 2], rr.at[J, 1], partner),
        )

    def forward(J, group, ssem, rslot, device):
        ref = block(J, group)
        return rcopy(ref, ref, ss.at[J, ssem], rr.at[J, rslot], device)

    def arrived(J, slot, group):
        ref = block(J, group)
        rcopy(ref, ref, ss.at[J, 0], rr.at[J, slot], partner).wait_recv()

    g_dn, g_up, g_far = pc.group(3, 0), pc.group(1, 0), pc.group(2, 0)

    def own(J):
        for copy in own_copies(J):
            copy.start()

    def stage_a(J):
        arrived(J, 2, g_dn)
        forward(J, g_dn, 3, 4, partner).start()

        @pl.when(J % 2 == 0)
        def _():
            forward(J, g_dn, 6, 6, up).start()

        arrived(J, 3, g_up)
        forward(J, g_up, 4, 5, partner).start()

        @pl.when(J % 2 == 1)
        def _():
            forward(J, g_up, 6, 6, down).start()

    def stage_b(J):
        @pl.when(J % 2 == 0)
        def _():
            arrived(J, 5, pc.group(1, 1))
            forward(J, pc.group(1, 1), 5, 7, down).start()

        @pl.when(J % 2 == 1)
        def _():
            arrived(J, 4, pc.group(3, 1))
            forward(J, pc.group(3, 1), 5, 7, up).start()

    def stage_c(J):
        @pl.when(J % 2 == 0)
        def _():
            arrived(J, 4, pc.group(3, 1))

        @pl.when(J % 2 == 1)
        def _():
            arrived(J, 5, pc.group(1, 1))

        arrived(J, 1, pc.group(0, 1))
        arrived(J, 6, g_far)
        arrived(J, 7, pc.group(2, 1))
        h, cols = part(J)
        even = h % 2
        x = xall[h, :, :, cols].reshape(NR, KCH)

        @pl.when(J % NCH == 0)
        def _():
            acc[even] = jnp.zeros(acc.shape[1:], F32)
            accm[even] = jnp.zeros(accm.shape[1:], F32)

        accm[even] += lax.dot_general(
            dn[:, cols], x, (((1,), (1,)), ((), ())), preferred_element_type=F32
        )
        acc[even] += jnp.dot(x, w[cols, :], preferred_element_type=F32)

    def table_copies(k, dy, flip):
        device = pc.peer(dy, flip)
        i = pc.group(dy, flip)
        qc = pl.ds(pl.multiple_of(i * QC, QC), QC)
        kc = pl.ds(pl.multiple_of(i * KVC, KVC), KVC)
        return (
            rcopy(uq.at[:, qc], uq_all.at[pc.g], ts.at[k, 0], tr.at[k, 0], device),
            rcopy(ukv.at[0, :, kc], uk_all.at[pc.g], ts.at[k, 1], tr.at[k, 1], device),
            rcopy(ukv.at[1, :, kc], uv_all.at[pc.g], ts.at[k, 2], tr.at[k, 2], device),
        )

    def late_copies():
        copies = [rcopy(uo_hbm, uo.at[pc.xl], ts.at[0, 4], tr.at[0, 4], partner)]
        for k, (dy, flip) in enumerate(PEERS):
            i = pc.group(dy, flip)
            qc = pl.ds(pl.multiple_of(i * QC, QC), QC)
            copies.append(
                rcopy(do.at[:, qc], do_all.at[pc.g], ts.at[k, 3], tr.at[k, 3], pc.peer(dy, flip))
            )
        return copies

    sub = lax.broadcasted_iota(jnp.int32, (HR, HD), 0)
    low = lax.broadcasted_iota(jnp.int32, (HR, HD), 1) < HD // 2

    def rotation(h, b):
        pos = 64 * (z * 4 + pc.quarter(b)) + HR * h + sub
        begin = jnp.zeros((HR, HD), jnp.int32)
        end = jnp.int32(0)
        for r in range(REQS):
            length = lens[b, r]
            end = end + length
            begin = begin + jnp.where(pos >= end, length, 0)
        angle = (pos - begin).astype(F32) * freq[...]
        rows = pl.ds(pl.multiple_of(h * NR + b * HR, HR), HR)
        cosb[rows, :] = jnp.cos(angle)
        sine = jnp.sin(angle)
        sinb[rows, :] = jnp.where(low, -sine, sine)

    def mid_copies(h):
        return [
            rcopy(midsend.at[h], mid_all.at[h, pc.g], ms.at[h, k], mr.at[h, k], pc.peer(*p))
            for k, p in enumerate(PEERS)
        ]

    def finish_mid(h):
        keep = (row_slots(pc, range(8), HR, HR * h, lens, adap, aslot) == pc.g).astype(F32)
        mid = (accm[h % 2] * keep).astype(BF16).reshape(3, RK, NR)
        midsend[h] = mid
        mid_all[h, pc.g] = mid
        for copy in mid_copies(h):
            copy.start()

    def kv_row(zsrc, quarter, h):
        return (zsrc * 4 + quarter) * H + h

    def z_copies(h, d):
        zd = (z + d) % 8
        device = pc.level(zd)
        return (
            rcopy(kvbuf.at[h, zd], kv_all.at[kv_row(z, pc.quarter(zd), h)], zs_s.at[h, d, 1], zs_r.at[h, d, 1], device),
            rcopy(qbuf.at[h, zd], q_all.at[z, h], zs_s.at[h, d, 0], zs_r.at[h, d, 0], device),
        )

    def finish_rows(h):
        for copy in mid_copies(h):
            copy.wait_recv()
        even = h % 2
        rows = pl.ds(pl.multiple_of(h * NR, NR), NR)
        cosv, sinv = cosb[rows, :], sinb[rows, :]

        def widen(which, table, base):
            mid = mid_all[h, :, which].reshape(8 * RK, NR)
            delta = lax.dot_general(
                mid, table[...].reshape(8 * RK, table.shape[2]), (((0,), (0,)), ((), ())),
                preferred_element_type=F32,
            )
            return base + 2.0 * delta

        def rope(v):
            return v * cosv + pltpu.roll(v, HD // 2, 1) * sinv

        key = rope(widen(1, uk_all, acc[even, :, QC : QC + KVC]))
        kvbuf[h, :, :, 0:HD] = key.astype(BF16).reshape(8, HR, HD)
        value = widen(2, uv_all, acc[even, :, QC + KVC : QC + 2 * KVC])
        kvbuf[h, :, :, HD : 2 * HD] = value.astype(BF16).reshape(8, HR, HD)
        kv_all[kv_row(z, q_own, h)] = kvbuf[h, z]
        for d in (4, 3, 5, 2, 6, 1, 7):
            z_copies(h, d)[0].start()
        query = widen(0, uq_all, acc[even, :, 0:QC])
        for j in range(4):
            qbuf[h, :, :, j * HD : (j + 1) * HD] = (
                rope(query[:, j * HD : (j + 1) * HD]).astype(BF16).reshape(8, HR, HD)
            )
        q_all[z, h] = qbuf[h, z]
        for d in (4, 3, 5, 2, 6, 1, 7):
            z_copies(h, d)[1].start()

    q_own = pc.quarter(z)
    q_across = (1 - q_own // 2) * 2 + pc.co
    xh_mate = jnp.where((z % 2) == pc.xl, pc.xh, (pc.xh + 1 - pc.co) % 2)
    q_mate = xh_mate * 2 + 1 - pc.co
    q_mate_across = (1 - xh_mate) * 2 + 1 - pc.co

    def kv_copy(quarter, h, d, k, device):
        ref = kv_all.at[kv_row((z + 8 - d) % 8, quarter, h)]
        return rcopy(ref, ref, gs.at[h, k, d], gr.at[h, k, d], device)

    def spread_own(h):
        def one(d, carry):
            @pl.when(d > 0)
            def _():
                z_copies(h, d)[0].wait_recv()

            kv_copy(q_own, h, d, 1, across).start()
            kv_copy(q_own, h, d, 0, mate).start()
            return carry

        lax.fori_loop(0, 8, one, None)

    def spread_across(h):
        def one(d, carry):
            kv_copy(q_across, h, d, 1, across).wait_recv()
            kv_copy(q_across, h, d, 2, mate).start()
            return carry

        lax.fori_loop(0, 8, one, None)

    def due(t, lag, run):
        last = t - lag

        @pl.when((last >= 0) & (last < NJ) & (last % NCH == NCH - 1))
        def _():
            run(last // NCH)

    def step(t, carry=None):
        @pl.when(t + LEAD < NJ)
        def _():
            own(t + LEAD)

        @pl.when(t < NJ)
        def _():
            stage_a(t)

        @pl.when((t >= LAG_B) & (t < NJ + LAG_B))
        def _():
            stage_b(t - LAG_B)

        @pl.when(t < NJ)
        def _():
            for i in range(8 // NCH):
                rotation(t // NCH, (t % NCH) * (8 // NCH) + i)

        @pl.when(t == LAG_C)
        def _():
            for k, p in enumerate(PEERS):
                for copy in table_copies(k, *p):
                    copy.wait_recv()

        @pl.when((t >= LAG_C) & (t < NJ + LAG_C))
        def _():
            stage_c(t - LAG_C)

        due(t, LAG_C, finish_mid)
        due(t, LAG_ROWS, finish_rows)
        due(t, LAG_OWN, spread_own)
        due(t, LAG_ACROSS, spread_across)
        return carry

    for J in range(LEAD):
        own(J)
    for k, p in enumerate(PEERS):
        for copy in table_copies(k, *p):
            copy.start()
    for load in loads:
        load.wait()
    lax.fori_loop(0, NJ + LAG_ACROSS, step, None)
    for copy in late_copies():
        copy.start()

    def collect(i, carry):
        h, d = i // 8, i % 8
        kv_copy(q_mate, h, d, 0, mate).wait_recv()
        kv_copy(q_mate_across, h, d, 2, mate).wait_recv()

        @pl.when(d > 0)
        def _():
            z_copies(h, d)[1].wait_recv()

        return carry

    lax.fori_loop(0, H * 8, collect, None)

    col = lax.broadcasted_iota(jnp.int32, (4 * BR, CK), 1)
    row1 = lax.broadcasted_iota(jnp.int32, (4 * BR, 1), 0) % BR
    scale = math.log2(math.e) / math.sqrt(HD)
    bk = CK // HR

    def offset_of(k):
        return 4 + jnp.where(k % 2 == 0, k // 2, -((k + 1) // 2))

    def back_copy(half, k):
        zd = (z + offset_of(k)) % 8
        return rcopy(att_buf.at[half, zd], att_all.at[half, z // 2, z % 2], as_.at[half, k], ar.at[half, k], pc.level(zd))

    def attend(it, carry):
        half, k = it // 8, it % 8
        zq = (z + offset_of(k)) % 8
        first = 64 * (zq * 4 + q_own) + BR * half
        pos = first + row1
        begin = jnp.zeros((4 * BR, 1), jnp.int32)
        end = jnp.int32(0)
        for r in range(REQS):
            length = lens[z, r]
            end = end + length
            begin = begin + jnp.where(pos >= end, length, 0)
        q = q_all[zq, pl.ds(half * (BR // HR), BR // HR)].reshape(BR, QC)
        q = jnp.concatenate([q[:, j * HD : (j + 1) * HD] for j in range(4)], axis=0)

        start = jnp.maximum(first + BR - NK * CK, 0)
        scores = []
        for i in range(NK):
            keys = kv_all[pl.ds(start // HR + i * bk, bk), :, 0:HD].reshape(CK, HD)
            s = lax.dot_general(q, keys, (((1,), (1,)), ((), ())), preferred_element_type=F32) * scale
            at = col + (start + i * CK)
            scores.append(jnp.where((at >= begin) & (at <= pos), s, NEG))
        top = functools.reduce(jnp.maximum, [jnp.max(s, axis=1, keepdims=True) for s in scores])
        total = jnp.zeros((4 * BR, 1), F32)
        accum = jnp.zeros((4 * BR, HD), F32)
        for i, s in enumerate(scores):
            values = kv_all[pl.ds(start // HR + i * bk, bk), :, HD : 2 * HD].reshape(CK, HD)
            p = jnp.exp2(s - top)
            total += jnp.sum(p, axis=1, keepdims=True)
            accum += jnp.dot(p.astype(BF16), values, preferred_element_type=F32)
        result = (accum / total).astype(BF16)
        for j in range(4):
            att_buf[half, zq, :, j * HD : (j + 1) * HD] = result[j * BR : (j + 1) * BR]

        @pl.when(k < 7)
        def _():
            back_copy(half, k).start()

        @pl.when(k == 7)
        def _():
            att_all[half, z // 2, z % 2] = att_buf[half, z]

        return carry

    def om_copy(half, k, dy, flip):
        to = pc.group(dy, flip)
        return rcopy(
            omsend.at[half, to % 2, to // 2], om_recv.at[half, pc.g], os_.at[half, k], or_.at[half, k],
            pc.peer(dy, flip),
        )

    def mid_send(half):
        for column in range(2):
            rows = att_all[half, :, column].reshape(4 * BR, QC)
            omsend[half, column] = lax.dot_general(
                do_all[...].reshape(8 * RK, QC), rows, (((1,), (1,)), ((), ())), preferred_element_type=F32
            ).reshape(4, 2 * RK, 4 * BR)
        for k, p in enumerate(PEERS):
            om_copy(half, k, *p).start()
        om_recv[half, pc.g] = omsend[half, pc.xl, pc.y]

    def mid_done(half):
        groups = [b * 2 + pc.xl for b in range(4)]
        slots = row_slots(pc, groups, BR, BR * half, lens, adap, aslot)
        mine = 2 * pc.y + lax.broadcasted_iota(jnp.int32, (2 * RK, 4 * BR), 0) // RK
        keep = (slots == mine).astype(F32)
        for k, p in enumerate(PEERS):
            om_copy(half, k, *p).wait_recv()
        om[half] = (jnp.sum(om_recv[half], axis=0) * keep).astype(BF16)

    def att_ready(half):
        for k in range(7):
            back_copy(half, k).wait_recv()

    y_far, y_up, y_dn = (pc.y + 2) % 4, (pc.y + 1) % 4, (pc.y + 3) % 4

    def x_copy(J):
        return rcopy(pbuf.at[J, :, 1 - pc.xl], xrecv.at[J], xs.at[J], xr.at[J], partner)

    def far_copy(J, odd):
        return rcopy(sbuf.at[J, y_far], far.at[J], ys.at[J, 0], yr.at[J, 0], down if odd else up)

    def up_copy(J):
        return rcopy(tup.at[J], rup.at[J], ys.at[J, 1], yr.at[J, 1], up)

    def dn_copy(J):
        return rcopy(tdn.at[J], rdn.at[J], ys.at[J, 2], yr.at[J, 2], down)

    def stage_p(J):
        half = J // NN
        cols = pl.ds(pl.multiple_of((J % NN) * NC, NC), NC)
        rows = att_all[half].reshape(8 * BR, QC)
        total = jnp.dot(rows, wo[:, cols], preferred_element_type=F32)
        pbuf[J] = total.astype(BF16).reshape(4, 2, BR, NC)
        x_copy(J).start()

    def stage_s(J, odd):
        half = J // NN
        cols = pl.ds(pl.multiple_of((J % NN) * NC, NC), NC)
        delta = lax.dot_general(
            om[half], uo[:, :, cols].reshape(2 * RK, NC), (((0,), (0,)), ((), ())), preferred_element_type=F32
        ).reshape(4, BR, NC)
        x_copy(J).wait_recv()
        total = pbuf[J, :, pc.xl].astype(F32) + xrecv[J].astype(F32) + 2.0 * delta
        sbuf[J] = total.astype(BF16)
        far_copy(J, odd).start()
        if odd:
            tup[J] = sbuf[J, y_up]
            up_copy(J).start()
        else:
            tdn[J] = sbuf[J, y_dn]
            dn_copy(J).start()

    def stage_t(J, odd):
        far_copy(J, odd).wait_recv()
        if odd:
            tdn[J] = (sbuf[J, y_dn].astype(F32) + far[J].astype(F32)).astype(BF16)
            dn_copy(J).start()
        else:
            tup[J] = (sbuf[J, y_up].astype(F32) + far[J].astype(F32)).astype(BF16)
            up_copy(J).start()

    def stage_f(J):
        up_copy(J).wait_recv()
        dn_copy(J).wait_recv()
        half = J // NN
        cols = pl.ds(pl.multiple_of((J % NN) * NC, NC), NC)
        total = sbuf[J, pc.y].astype(F32) + rup[J].astype(F32) + rdn[J].astype(F32)
        out[pl.ds(pl.multiple_of(half * BR, BR), BR), cols] = total

    def turn(t, carry=None):
        @pl.when((t >= 1) & (t < NT // 2 + 1))
        def _():
            stage_s(2 * t - 2, False)
            stage_s(2 * t - 1, True)

        @pl.when((t >= 2) & (t < NT // 2 + 2))
        def _():
            stage_t(2 * t - 4, False)
            stage_t(2 * t - 3, True)

        @pl.when(t >= 3)
        def _():
            stage_f(2 * t - 6)
            stage_f(2 * t - 5)

        return carry

    lax.fori_loop(0, 16, attend, None)
    for copy in late_copies():
        copy.wait_recv()
    att_ready(0)
    mid_send(0)

    def whole(t, carry):
        @pl.when(t < NT // 2)
        def _():
            stage_p(2 * t)
            stage_p(2 * t + 1)

        @pl.when(t == 0)
        def _():
            mid_done(0)

        @pl.when(t == NN // 2 - 2)
        def _():
            att_ready(1)
            mid_send(1)

        @pl.when(t == NN // 2)
        def _():
            mid_done(1)

        return turn(t, carry)

    lax.fori_loop(0, NT // 2 + 3, whole, None)

    def drain_z(i, carry):
        h, d = i // 8, i % 8

        @pl.when(d > 0)
        def _():
            kv, q = z_copies(h, d)
            kv.wait_send()
            q.wait_send()

        kv_copy(q_own, h, d, 1, across).wait_send()
        kv_copy(q_own, h, d, 0, mate).wait_send()
        kv_copy(q_across, h, d, 2, mate).wait_send()
        return carry

    lax.fori_loop(0, H * 8, drain_z, None)

    def drain_mid(h, carry):
        for copy in mid_copies(h):
            copy.wait_send()
        return carry

    lax.fori_loop(0, H, drain_mid, None)

    def drain_back(half, carry):
        for k in range(7):
            back_copy(half, k).wait_send()
        for k, p in enumerate(PEERS):
            om_copy(half, k, *p).wait_send()
        return carry

    lax.fori_loop(0, 2, drain_back, None)
    for k, p in enumerate(PEERS):
        for copy in table_copies(k, *p):
            copy.wait_send()
    for copy in late_copies():
        copy.wait_send()

    def drain_tok(J, carry):
        for copy in own_copies(J):
            copy.wait_send()
        for k in range(3, 7):
            forward(J, pc.g, k, 0, partner).wait_send()
        return carry

    lax.fori_loop(0, NJ, drain_tok, None)

    def drain_out(J, carry):
        x_copy(J).wait_send()
        far_copy(J, False).wait_send()
        up_copy(J).wait_send()
        dn_copy(J).wait_send()
        return carry

    lax.fori_loop(0, NT, drain_out, None)


def layer(*args):
    any_ = pl.BlockSpec(memory_space=pl.ANY)
    vmem = pl.BlockSpec(memory_space=pltpu.VMEM)
    smem = pl.BlockSpec(memory_space=pltpu.SMEM)
    dma = pltpu.SemaphoreType.DMA
    return pl.pallas_call(
        layer_kernel,
        name="layer",
        out_shape=jax.ShapeDtypeStruct((64, D), F32),
        in_specs=[smem] * 3 + [any_] * 10 + [vmem],
        out_specs=vmem,
        scratch_shapes=[
            pltpu.VMEM((H, 8, HR, D), BF16),
            pltpu.VMEM((D, QC + 2 * KVC), BF16),
            pltpu.VMEM((QC, D), BF16),
            pltpu.VMEM((3 * RK, D), BF16),
            pltpu.VMEM((2, RK, D), BF16),
            pltpu.VMEM((2, NR, QC + 2 * KVC), F32),
            pltpu.VMEM((2, 3 * RK, NR), F32),
            pltpu.VMEM((8, RK, QC), BF16),
            pltpu.VMEM((8, RK, KVC), BF16),
            pltpu.VMEM((8, RK, KVC), BF16),
            pltpu.VMEM((8, RK, QC), BF16),
            pltpu.VMEM((H, 3, RK, NR), BF16),
            pltpu.VMEM((H, 8, 3, RK, NR), BF16),
            pltpu.VMEM((H, 8, HR, QC), BF16),
            pltpu.VMEM((H, 8, HR, 2 * HD), BF16),
            pltpu.VMEM((512, HD), F32),
            pltpu.VMEM((512, HD), F32),
            pltpu.VMEM((8, H, HR, QC), BF16),
            pltpu.VMEM((32 * H, HR, 2 * HD), BF16),
            pltpu.VMEM((2, 8, BR, QC), BF16),
            pltpu.VMEM((2, 4, 2, BR, QC), BF16),
            pltpu.VMEM((2, 2, 4, 2 * RK, 4 * BR), F32),
            pltpu.VMEM((2, 8, 2 * RK, 4 * BR), F32),
            pltpu.VMEM((2, 2 * RK, 4 * BR), BF16),
            pltpu.VMEM((NT, 4, 2, BR, NC), BF16),
            pltpu.VMEM((NT, 4, BR, NC), BF16),
            pltpu.VMEM((NT, 4, BR, NC), BF16),
            pltpu.VMEM((NT, BR, NC), BF16),
            pltpu.VMEM((NT, BR, NC), BF16),
            pltpu.VMEM((NT, BR, NC), BF16),
            pltpu.VMEM((NT, BR, NC), BF16),
            pltpu.VMEM((NT, BR, NC), BF16),
            dma((10 + H,)),
            dma((7, 5)),
            dma((7, 5)),
            dma((NJ, 7)),
            dma((NJ, 8)),
            dma((H, 7)),
            dma((H, 7)),
            dma((H, 8, 2)),
            dma((H, 8, 2)),
            dma((H, 3, 8)),
            dma((H, 3, 8)),
            dma((2, 8)),
            dma((2, 8)),
            dma((2, 7)),
            dma((2, 7)),
            dma((NT,)),
            dma((NT,)),
            dma((NT, 3)),
            dma((NT, 3)),
        ],
        compiler_params=pltpu.CompilerParams(
            collective_id=0, has_side_effects=True, vmem_limit_bytes=61 << 20
        ),
    )(*args)


def body(
    tokens, req_lengths, req_adapter, adapter_slot, query_weight, key_weight, value_weight, w_out,
    down_qkv, up_query, up_kv, down_out, up_out,
):
    half = np.arange(HD) % (HD // 2)
    freq = jnp.asarray(np.exp(half * (-2.0 * math.log(ROPE_BASE) / HD)).astype(np.float32)[None, :])
    out = layer(
        req_lengths, req_adapter, adapter_slot, tokens[0], query_weight, key_weight, value_weight, w_out,
        down_qkv[0], up_query[0], up_kv[0], down_out[0], up_out[0], freq,
    )
    return out.astype(BF16)[None]


def solution(mesh):
    placed = (
        P("grp", "ctx", None),
        P(),
        P(),
        P(),
        P(None, "grp"),
        P(None, "grp"),
        P(None, "grp"),
        P("grp", None),
        P("grp", None, None),
        P("grp", None, None),
        P("grp", None, None, None),
        P("grp", None, None),
        P("grp", None, None),
    )
    return jax.shard_map(
        body, mesh=mesh, in_specs=placed, out_specs=P("grp", "ctx", None), check_vma=False
    )
```

```python
import functools
import math

import jax
import jax.numpy as jnp
import numpy as np
from jax import lax
from jax.experimental import pallas as pl
from jax.experimental.pallas import tpu as pltpu
from jax.sharding import PartitionSpec as P

D = 4096
HD = 128
RK = 16
REQS = 8
ROPE_BASE = 500000.0
MESH = pl.DeviceIdType.MESH
F32 = jnp.float32
BF16 = jnp.bfloat16
NEG = -1e30

QC = 512
KVC = 128
H = 4
HR = 64 // H
NR = 8 * HR
NCH = 2
KCH = D // NCH
NJ = H * NCH
LEAD = 4
LAG_B, LAG_C, LAG_ROWS, LAG_OWN, LAG_ACROSS = 2, 5, 5+2, 5+4, 5+5
BR = 32
CK = 384
NK = -(-(1088 + BR - 1) // CK)
NC = 512
NN = D // NC
NT = 2 * NN
READY = 11


class Place:
    def __init__(self):
        self.g = lax.axis_index("grp")
        self.c = lax.axis_index("ctx")
        self.y = self.g // 2
        self.xl = self.g % 2
        self.z = self.c // 4
        self.xh = (self.c // 2) % 2
        self.co = self.c % 2
        self.xh2 = (self.xh + self.co) % 2

    def group(self, dy, flip):
        return ((self.y + dy) % 4) * 2 + (self.xl + flip) % 2

    def peer(self, dy, flip):
        ctx = self.z * 4 + self.xh2 * 2 + self.co if flip else self.c
        return (self.group(dy, flip), ctx)

    def level(self, z):
        return (self.g, z * 4 + self.xh * 2 + self.co)

    def quarter(self, b):
        xh = jnp.where((b % 2) == self.xl, self.xh, self.xh2)
        return xh * 2 + self.co


PEERS = [(dy, flip) for dy in range(4) for flip in range(2)][1:]


def rcopy(src, dst, ssem, rsem, device):
    return pltpu.make_async_remote_copy(
        src_ref=src, dst_ref=dst, send_sem=ssem, recv_sem=rsem, device_id=device, device_id_type=MESH
    )


def take(ref, sem):
    pltpu.make_async_copy(ref, ref, sem).wait()


def greet(devices):
    barrier = pltpu.get_barrier_semaphore()
    for device in devices:
        pl.semaphore_signal(barrier, inc=1, device_id=device, device_id_type=MESH)
    pl.semaphore_wait(barrier, len(devices))


def row_slots(place, groups, rows, offset, lens, adap, aslot):
    lane = lax.broadcasted_iota(jnp.int32, (8, len(groups) * rows), 1)
    out = jnp.zeros(lane.shape, jnp.int32)
    for i, b in enumerate(groups):
        pos = 64 * (place.z * 4 + place.quarter(b)) + offset + lane - i * rows
        mine = (lane >= i * rows) & (lane < (i + 1) * rows)
        end = jnp.int32(0)
        for r in range(REQS):
            begin = end
            end = begin + lens[b, r]
            hit = mine & (pos >= begin) & (pos < end)
            out = jnp.where(hit, aslot[adap[b, r]], out)
    return out[0:1, :]


def layer_kernel(
    lens, adap, aslot, tok, wq, wk, wv, w_out, dn_hbm, uq, ukv, do, uo_hbm, freq,
    out,
    xall, w, wo, dn, uo, acc, accm, uq_all, uk_all, uv_all, do_all, midsend, mid_all, qbuf, kvbuf,
    cosb, sinb, q_all, kv_all, att_buf, att_all, omsend, om_recv, om, pbuf, xrecv, sbuf, far, tup, tdn, rup, rdn,
    lsem, sent, tr, rr, mr, zr, gr, ar, orr, xr, yr,
):
    pc = Place()
    z = pc.z
    partner = pc.peer(0, 1)
    up = pc.peer(1, 0)
    down = pc.peer(3, 0)
    mate = (pc.g, z * 4 + pc.xh * 2 + 1 - pc.co)
    across = (pc.g, z * 4 + (1 - pc.xh) * 2 + pc.co)
    qcols = pl.ds(pl.multiple_of(pc.g * QC, QC), QC)
    kcols = pl.ds(pl.multiple_of(pc.g * KVC, KVC), KVC)

    local = [(tok.at[h * HR : (h + 1) * HR, :], xall.at[h, pc.g]) for h in range(H)] + [
        (wq, w.at[:, 0:QC]),
        (wk, w.at[:, QC : QC + KVC]),
        (wv, w.at[:, QC + KVC : QC + 2 * KVC]),
        (dn_hbm, dn),
        (uq.at[:, qcols], uq_all.at[pc.g]),
        (ukv.at[0, :, kcols], uk_all.at[pc.g]),
        (ukv.at[1, :, kcols], uv_all.at[pc.g]),
        (do.at[:, qcols], do_all.at[pc.g]),
        (uo_hbm, uo.at[pc.xl]),
        (w_out, wo),
    ]
    loads = [pltpu.make_async_copy(src, dst, lsem.at[i]) for i, (src, dst) in enumerate(local)]
    for load in loads:
        load.start()

    greet(
        [pc.peer(*p) for p in PEERS]
        + [pc.level((z + d) % 8) for d in range(1, 8)]
        + [mate, across]
    )

    def part(J):
        return J // NCH, pl.ds(pl.multiple_of((J % NCH) * KCH, KCH), KCH)

    def block(J, group):
        h, cols = part(J)
        return xall.at[h, group, :, cols]

    def own_copies(J):
        src = dst = block(J, pc.g)
        return (
            rcopy(src, dst, sent.at[0], rr.at[J, 0], up),
            rcopy(src, dst, sent.at[0], rr.at[J, 1], down),
            rcopy(src, dst, sent.at[0], rr.at[J, 3], partner),
        )

    def forward(J, group, wave, device):
        ref = block(J, group)
        return rcopy(ref, ref, sent.at[0], rr.at[J, wave], device)

    def arrived(J, wave, blocks=1):
        h, cols = part(J)
        take(xall.at[h, 0:blocks, :, cols], rr.at[J, wave])

    g_dn, g_up = pc.group(3, 0), pc.group(1, 0)

    def own(J):
        for copy in own_copies(J):
            copy.start()

    def stage_a(J):
        even = J % 2 == 0
        arrived(J, 0)

        @pl.when(even)
        def _():
            forward(J, g_dn, 3, partner).start()
            forward(J, g_dn, 3, up).start()

        @pl.when(J % 2 == 1)
        def _():
            forward(J, g_dn, 2, partner).start()

        arrived(J, 1)

        @pl.when(even)
        def _():
            forward(J, g_up, 2, partner).start()

        @pl.when(J % 2 == 1)
        def _():
            forward(J, g_up, 3, partner).start()
            forward(J, g_up, 3, down).start()

    def stage_b(J):
        arrived(J, 2)

        @pl.when(J % 2 == 0)
        def _():
            forward(J, pc.group(1, 1), 3, down).start()

        @pl.when(J % 2 == 1)
        def _():
            forward(J, pc.group(3, 1), 3, up).start()

    def stage_c(J):
        arrived(J, 3, 4)
        h, cols = part(J)
        even = h % 2
        x = xall[h, :, :, cols].reshape(NR, KCH)

        @pl.when(J % NCH == 0)
        def _():
            acc[even] = jnp.zeros(acc.shape[1:], F32)
            accm[even] = jnp.zeros(accm.shape[1:], F32)

        accm[even] += lax.dot_general(
            dn[:, cols], x, (((1,), (1,)), ((), ())), preferred_element_type=F32
        )
        acc[even] += jnp.dot(x, w[cols, :], preferred_element_type=F32)

    def table_copies(k, dy, flip):
        device = pc.peer(dy, flip)
        i = pc.group(dy, flip)
        qc = pl.ds(pl.multiple_of(i * QC, QC), QC)
        kc = pl.ds(pl.multiple_of(i * KVC, KVC), KVC)
        return (
            rcopy(uq.at[:, qc], uq_all.at[pc.g], sent.at[1], tr.at[0], device),
            rcopy(ukv.at[0, :, kc], uk_all.at[pc.g], sent.at[2], tr.at[1], device),
            rcopy(ukv.at[1, :, kc], uv_all.at[pc.g], sent.at[3], tr.at[2], device),
        )

    def late_copies():
        copies = [rcopy(uo_hbm, uo.at[pc.xl], sent.at[5], tr.at[4], partner)]
        for k, (dy, flip) in enumerate(PEERS):
            i = pc.group(dy, flip)
            qc = pl.ds(pl.multiple_of(i * QC, QC), QC)
            copies.append(
                rcopy(do.at[:, qc], do_all.at[pc.g], sent.at[4], tr.at[3], pc.peer(dy, flip))
            )
        return copies

    sub = lax.broadcasted_iota(jnp.int32, (HR, HD), 0)
    low = lax.broadcasted_iota(jnp.int32, (HR, HD), 1) < HD // 2

    def rotation(h, b):
        pos = 64 * (z * 4 + pc.quarter(b)) + HR * h + sub
        begin = jnp.zeros((HR, HD), jnp.int32)
        end = jnp.int32(0)
        for r in range(REQS):
            length = lens[b, r]
            end = end + length
            begin = begin + jnp.where(pos >= end, length, 0)
        angle = (pos - begin).astype(F32) * freq[...]
        rows = pl.ds(pl.multiple_of(h * NR + b * HR, HR), HR)
        cosb[rows, :] = jnp.cos(angle)
        sine = jnp.sin(angle)
        sinb[rows, :] = jnp.where(low, -sine, sine)

    def mid_copies(h):
        return [
            rcopy(midsend.at[h], mid_all.at[h, pc.g], sent.at[6], mr.at[h], pc.peer(*p))
            for k, p in enumerate(PEERS)
        ]

    def finish_mid(h):
        keep = (row_slots(pc, range(8), HR, HR * h, lens, adap, aslot) == pc.g).astype(F32)
        mid = (accm[h % 2] * keep).astype(BF16).reshape(3, RK, NR)
        midsend[h] = mid
        mid_all[h, pc.g] = mid
        for copy in mid_copies(h):
            copy.start()

    def kv_row(zsrc, quarter, h):
        return (zsrc * 4 + quarter) * H + h

    def z_copies(h, d):
        zd = (z + d) % 8
        device = pc.level(zd)
        return (
            rcopy(kvbuf.at[h, zd], kv_all.at[kv_row(z, pc.quarter(zd), h)], sent.at[7], zr.at[h], device),
            rcopy(qbuf.at[h, zd], q_all.at[z, h], sent.at[8], zr.at[H], device),
        )

    def finish_rows(h):
        take(mid_all.at[h, 0:7], mr.at[h])
        even = h % 2
        rows = pl.ds(pl.multiple_of(h * NR, NR), NR)
        cosv, sinv = cosb[rows, :], sinb[rows, :]

        def widen(which, table, base):
            mid = mid_all[h, :, which].reshape(8 * RK, NR)
            delta = lax.dot_general(
                mid, table[...].reshape(8 * RK, table.shape[2]), (((0,), (0,)), ((), ())),
                preferred_element_type=F32,
            )
            return base + 2.0 * delta

        def rope(v):
            return v * cosv + pltpu.roll(v, HD // 2, 1) * sinv

        key = rope(widen(1, uk_all, acc[even, :, QC : QC + KVC]))
        kvbuf[h, :, :, 0:HD] = key.astype(BF16).reshape(8, HR, HD)
        value = widen(2, uv_all, acc[even, :, QC + KVC : QC + 2 * KVC])
        kvbuf[h, :, :, HD : 2 * HD] = value.astype(BF16).reshape(8, HR, HD)
        kv_all[kv_row(z, q_own, h)] = kvbuf[h, z]
        for d in (4, 3, 5, 2, 6, 1, 7):
            z_copies(h, d)[0].start()
        query = widen(0, uq_all, acc[even, :, 0:QC])
        for j in range(4):
            qbuf[h, :, :, j * HD : (j + 1) * HD] = (
                rope(query[:, j * HD : (j + 1) * HD]).astype(BF16).reshape(8, HR, HD)
            )
        q_all[z, h] = qbuf[h, z]
        for d in (4, 3, 5, 2, 6, 1, 7):
            z_copies(h, d)[1].start()

    q_own = pc.quarter(z)
    q_across = (1 - q_own // 2) * 2 + pc.co
    xh_mate = jnp.where((z % 2) == pc.xl, pc.xh, (pc.xh + 1 - pc.co) % 2)
    q_mate = xh_mate * 2 + 1 - pc.co
    q_mate_across = (1 - xh_mate) * 2 + 1 - pc.co

    def kv_copy(quarter, h, d, k, device):
        ref = kv_all.at[kv_row((z + 8 - d) % 8, quarter, h)]
        return rcopy(ref, ref, sent.at[9], gr.at[jnp.where(k == 1, h, H + k // 2)], device)

    def spread_own(h):
        take(kv_all.at[0:7], zr.at[h])

        def one(d, carry):
            kv_copy(q_own, h, d, 1, across).start()
            kv_copy(q_own, h, d, 0, mate).start()
            return carry

        lax.fori_loop(0, 8, one, None)

    def spread_across(h):
        take(kv_all.at[0:8], gr.at[h])

        def one(d, carry):
            kv_copy(q_across, h, d, 2, mate).start()
            return carry

        lax.fori_loop(0, 8, one, None)

    def due(t, lag, run):
        last = t - lag

        @pl.when((last >= 0) & (last < NJ) & (last % NCH == NCH - 1))
        def _():
            run(last // NCH)

    def step(t, carry=None):
        @pl.when(t + LEAD < NJ)
        def _():
            own(t + LEAD)

        @pl.when(t < NJ)
        def _():
            stage_a(t)

        @pl.when((t >= LAG_B) & (t < NJ + LAG_B))
        def _():
            stage_b(t - LAG_B)

        @pl.when(t < NJ)
        def _():
            for i in range(8 // NCH):
                rotation(t // NCH, (t % NCH) * (8 // NCH) + i)

        @pl.when(t == LAG_C)
        def _():
            for i, table in enumerate((uq_all, uk_all, uv_all)):
                take(table.at[0:7], tr.at[i])

        @pl.when((t >= LAG_C) & (t < NJ + LAG_C))
        def _():
            stage_c(t - LAG_C)

        due(t, LAG_C, finish_mid)
        due(t, LAG_ROWS, finish_rows)
        due(t, LAG_OWN, spread_own)
        due(t, LAG_ACROSS, spread_across)
        return carry

    for load in loads[:H]:
        load.wait()
    for J in range(LEAD):
        own(J)
    for k, p in enumerate(PEERS):
        for copy in table_copies(k, *p):
            copy.start()
    for load in loads[H:]:
        load.wait()
    lax.fori_loop(0, NJ + LAG_ACROSS, step, None)
    for copy in late_copies():
        copy.start()

    take(q_all.at[0:7], zr.at[H])
    for k in range(2):
        take(kv_all.at[0 : 8 * H], gr.at[H + k])

    col = lax.broadcasted_iota(jnp.int32, (4 * BR, CK), 1)
    row1 = lax.broadcasted_iota(jnp.int32, (4 * BR, 1), 0) % BR
    scale = math.log2(math.e) / math.sqrt(HD)
    bk = CK // HR

    def offset_of(k):
        return 4 + jnp.where(k % 2 == 0, k // 2, -((k + 1) // 2))

    def back_copy(half, k):
        zd = (z + offset_of(k)) % 8
        return rcopy(att_buf.at[half, zd], att_all.at[half, z // 2, z % 2], sent.at[10], ar.at[half], pc.level(zd))

    def attend(it, carry):
        half, k = it // 8, it % 8
        zq = (z + offset_of(k)) % 8
        first = 64 * (zq * 4 + q_own) + BR * half
        pos = first + row1
        begin = jnp.zeros((4 * BR, 1), jnp.int32)
        end = jnp.int32(0)
        for r in range(REQS):
            length = lens[z, r]
            end = end + length
            begin = begin + jnp.where(pos >= end, length, 0)
        q = q_all[zq, pl.ds(half * (BR // HR), BR // HR)].reshape(BR, QC)
        q = jnp.concatenate([q[:, j * HD : (j + 1) * HD] for j in range(4)], axis=0)

        start = jnp.maximum(first + BR - NK * CK, 0)
        scores = []
        for i in range(NK):
            keys = kv_all[pl.ds(start // HR + i * bk, bk), :, 0:HD].reshape(CK, HD)
            s = lax.dot_general(q, keys, (((1,), (1,)), ((), ())), preferred_element_type=F32) * scale
            at = col + (start + i * CK)
            scores.append(jnp.where((at >= begin) & (at <= pos), s, NEG))
        top = functools.reduce(jnp.maximum, [jnp.max(s, axis=1, keepdims=True) for s in scores])
        total = jnp.zeros((4 * BR, 1), F32)
        accum = jnp.zeros((4 * BR, HD), F32)
        for i, s in enumerate(scores):
            values = kv_all[pl.ds(start // HR + i * bk, bk), :, HD : 2 * HD].reshape(CK, HD)
            p = jnp.exp2(s - top)
            total += jnp.sum(p, axis=1, keepdims=True)
            accum += jnp.dot(p.astype(BF16), values, preferred_element_type=F32)
        result = (accum / total).astype(BF16)
        for j in range(4):
            att_buf[half, zq, :, j * HD : (j + 1) * HD] = result[j * BR : (j + 1) * BR]

        @pl.when(k < 7)
        def _():
            back_copy(half, k).start()

        @pl.when(k == 7)
        def _():
            att_all[half, z // 2, z % 2] = att_buf[half, z]

        return carry

    def om_copy(half, k, dy, flip):
        to = pc.group(dy, flip)
        return rcopy(
            omsend.at[half, to % 2, to // 2], om_recv.at[half, pc.g], sent.at[11], orr.at[half],
            pc.peer(dy, flip),
        )

    def mid_send(half):
        for column in range(2):
            rows = att_all[half, :, column].reshape(4 * BR, QC)
            omsend[half, column] = lax.dot_general(
                do_all[...].reshape(8 * RK, QC), rows, (((1,), (1,)), ((), ())), preferred_element_type=F32
            ).reshape(4, 2 * RK, 4 * BR)
        for k, p in enumerate(PEERS):
            om_copy(half, k, *p).start()
        om_recv[half, pc.g] = omsend[half, pc.xl, pc.y]

    def mid_done(half):
        groups = [b * 2 + pc.xl for b in range(4)]
        slots = row_slots(pc, groups, BR, BR * half, lens, adap, aslot)
        mine = 2 * pc.y + lax.broadcasted_iota(jnp.int32, (2 * RK, 4 * BR), 0) // RK
        keep = (slots == mine).astype(F32)
        take(om_recv.at[half, 0:7], orr.at[half])
        om[half] = (jnp.sum(om_recv[half], axis=0) * keep).astype(BF16)

    def att_ready(half):
        take(att_buf.at[half, 0:7], ar.at[half])

    y_far, y_up, y_dn = (pc.y + 2) % 4, (pc.y + 1) % 4, (pc.y + 3) % 4

    def x_copy(J):
        return rcopy(pbuf.at[J, :, 1 - pc.xl], xrecv.at[J], sent.at[12], xr.at[J // 2], partner)

    def far_copy(J, odd):
        return rcopy(sbuf.at[J, y_far], far.at[J], sent.at[13], yr.at[J // 2, 0], down if odd else up)

    def up_copy(J):
        return rcopy(tup.at[J], rup.at[J], sent.at[14], yr.at[J // 2, 1], up)

    def dn_copy(J):
        return rcopy(tdn.at[J], rdn.at[J], sent.at[15], yr.at[J // 2, 1], down)

    def stage_p(J):
        half = J // NN
        cols = pl.ds(pl.multiple_of((J % NN) * NC, NC), NC)
        rows = att_all[half].reshape(8 * BR, QC)
        total = jnp.dot(rows, wo[:, cols], preferred_element_type=F32)
        pbuf[J] = total.astype(BF16).reshape(4, 2, BR, NC)
        x_copy(J).start()

    def stage_s(J, odd):
        half = J // NN
        cols = pl.ds(pl.multiple_of((J % NN) * NC, NC), NC)
        delta = lax.dot_general(
            om[half], uo[:, :, cols].reshape(2 * RK, NC), (((0,), (0,)), ((), ())), preferred_element_type=F32
        ).reshape(4, BR, NC)
        total = pbuf[J, :, pc.xl].astype(F32) + xrecv[J].astype(F32) + 2.0 * delta
        sbuf[J] = total.astype(BF16)
        far_copy(J, odd).start()
        if odd:
            tup[J] = sbuf[J, y_up]
            up_copy(J).start()
        else:
            tdn[J] = sbuf[J, y_dn]
            dn_copy(J).start()

    def stage_t(J, odd):
        if odd:
            tdn[J] = (sbuf[J, y_dn].astype(F32) + far[J].astype(F32)).astype(BF16)
            dn_copy(J).start()
        else:
            tup[J] = (sbuf[J, y_up].astype(F32) + far[J].astype(F32)).astype(BF16)
            up_copy(J).start()

    def stage_f(J):
        half = J // NN
        cols = pl.ds(pl.multiple_of((J % NN) * NC, NC), NC)
        total = sbuf[J, pc.y].astype(F32) + rup[J].astype(F32) + rdn[J].astype(F32)
        out[pl.ds(pl.multiple_of(half * BR, BR), BR), cols] = total

    HP = NN // 2

    def pair_p(u):
        stage_p(2 * u)
        stage_p(2 * u + 1)

    def attend_and_project(it, carry):
        attend(it, carry)

        @pl.when(it == READY)
        def _():
            take(do_all.at[0:7], tr.at[3])
            take(uo.at[0], tr.at[4])
            att_ready(0)
            mid_send(0)

        @pl.when((it >= READY) & (it < READY + HP))
        def _():
            pair_p(it - READY)

        return carry

    lax.fori_loop(0, 16, attend_and_project, None)
    mid_done(0)

    def reduce(t, carry):
        @pl.when(t == HP)
        def _():
            mid_done(1)

        @pl.when(t < 2 * HP)
        def _():
            take(xrecv.at[0:2], xr.at[t])
            stage_s(2 * t, False)
            stage_s(2 * t + 1, True)

        @pl.when((t >= 1) & (t < 2 * HP + 1))
        def _():
            take(far.at[0:2], yr.at[t - 1, 0])
            stage_t(2 * t - 2, False)
            stage_t(2 * t - 1, True)

        @pl.when(t >= 2)
        def _():
            take(rup.at[0:4], yr.at[t - 2, 1])
            stage_f(2 * t - 4)
            stage_f(2 * t - 3)

        @pl.when(t == 1)
        def _():
            att_ready(1)
            mid_send(1)
            pair_p(HP)

        @pl.when((t >= 1) & (t < HP))
        def _():
            pair_p(t + HP)

        return carry

    lax.fori_loop(0, 2 * HP + 2, reduce, None)

    for i, ref in enumerate(
        (
            xall.at[:, 0:7], uq_all.at[0:7], uk_all.at[0:7], uv_all.at[0:7], do_all.at[0:7], uo.at[0],
            mid_all.at[:, 0:7], kvbuf.at[:, 0:7], qbuf.at[:, 0:7], kv_all.at[0 : 24 * H],
            att_buf.at[:, 0:7], om_recv.at[:, 0:7], xrecv, far, rup, rdn,
        )
    ):
        take(ref, sent.at[i])


def layer(*args):
    any_ = pl.BlockSpec(memory_space=pltpu.HBM)
    vmem = pl.BlockSpec(memory_space=pltpu.VMEM)
    smem = pl.BlockSpec(memory_space=pltpu.SMEM)
    dma = pltpu.SemaphoreType.DMA
    return pl.pallas_call(
        layer_kernel,
        name="layer",
        out_shape=jax.ShapeDtypeStruct((64, D), F32),
        in_specs=[smem] * 3 + [any_] * 10 + [vmem],
        out_specs=vmem,
        scratch_shapes=[
            pltpu.VMEM((H, 8, HR, D), BF16),
            pltpu.VMEM((D, QC + 2 * KVC), BF16),
            pltpu.VMEM((QC, D), BF16),
            pltpu.VMEM((3 * RK, D), BF16),
            pltpu.VMEM((2, RK, D), BF16),
            pltpu.VMEM((2, NR, QC + 2 * KVC), F32),
            pltpu.VMEM((2, 3 * RK, NR), F32),
            pltpu.VMEM((8, RK, QC), BF16),
            pltpu.VMEM((8, RK, KVC), BF16),
            pltpu.VMEM((8, RK, KVC), BF16),
            pltpu.VMEM((8, RK, QC), BF16),
            pltpu.VMEM((H, 3, RK, NR), BF16),
            pltpu.VMEM((H, 8, 3, RK, NR), BF16),
            pltpu.VMEM((H, 8, HR, QC), BF16),
            pltpu.VMEM((H, 8, HR, 2 * HD), BF16),
            pltpu.VMEM((512, HD), F32),
            pltpu.VMEM((512, HD), F32),
            pltpu.VMEM((8, H, HR, QC), BF16),
            pltpu.VMEM((32 * H, HR, 2 * HD), BF16),
            pltpu.VMEM((2, 8, BR, QC), BF16),
            pltpu.VMEM((2, 4, 2, BR, QC), BF16),
            pltpu.VMEM((2, 2, 4, 2 * RK, 4 * BR), F32),
            pltpu.VMEM((2, 8, 2 * RK, 4 * BR), F32),
            pltpu.VMEM((2, 2 * RK, 4 * BR), BF16),
            pltpu.VMEM((NT, 4, 2, BR, NC), BF16),
            pltpu.VMEM((NT, 4, BR, NC), BF16),
            pltpu.VMEM((NT, 4, BR, NC), BF16),
            pltpu.VMEM((NT, BR, NC), BF16),
            pltpu.VMEM((NT, BR, NC), BF16),
            pltpu.VMEM((NT, BR, NC), BF16),
            pltpu.VMEM((NT, BR, NC), BF16),
            pltpu.VMEM((NT, BR, NC), BF16),
            dma((10 + H,)),
            dma((16,)),
            dma((5,)),
            dma((NJ, 4)),
            dma((H,)),
            dma((H + 1,)),
            dma((H + 2,)),
            dma((2,)),
            dma((2,)),
            dma((NT // 2,)),
            dma((NT // 2, 2)),
        ],
        compiler_params=pltpu.CompilerParams(
            collective_id=0, has_side_effects=True, vmem_limit_bytes=61 << 20
        ),
    )(*args)


def body(
    tokens, req_lengths, req_adapter, adapter_slot, query_weight, key_weight, value_weight, w_out,
    down_qkv, up_query, up_kv, down_out, up_out,
):
    half = np.arange(HD) % (HD // 2)
    freq = jnp.asarray(np.exp(half * (-2.0 * math.log(ROPE_BASE) / HD)).astype(np.float32)[None, :])
    out = layer(
        req_lengths, req_adapter, adapter_slot, tokens[0], query_weight, key_weight, value_weight, w_out,
        down_qkv[0], up_query[0], up_kv[0], down_out[0], up_out[0], freq,
    )
    return out.astype(BF16)[None]


def solution(mesh):
    placed = (
        P("grp", "ctx", None),
        P(),
        P(),
        P(),
        P(None, "grp"),
        P(None, "grp"),
        P(None, "grp"),
        P("grp", None),
        P("grp", None, None),
        P("grp", None, None),
        P("grp", None, None, None),
        P("grp", None, None),
        P("grp", None, None),
    )
    return jax.shard_map(
        body, mesh=mesh, in_specs=placed, out_specs=P("grp", "ctx", None), check_vma=False
    )
```

```python
import functools
import math

import jax
import jax.numpy as jnp
import numpy as np
from jax import lax
from jax.experimental import pallas as pl
from jax.experimental.pallas import tpu as pltpu
from jax.sharding import PartitionSpec as P

D = 4096
HD = 128
RK = 16
REQS = 8
ROPE_BASE = 500000.0
MESH = pl.DeviceIdType.MESH
F32 = jnp.float32
BF16 = jnp.bfloat16
NEG = -1e30

QC = 512
KVC = 128
H = 2
HR = 64 // H
NR = 8 * HR
NCH = 4
KCH = D // NCH
NJ = H * NCH
LEAD = 4
LAG_B, LAG_C, LAG_ROWS, LAG_OWN, LAG_ACROSS = 2, 5, 5+2, 5+4, 5+5
BR = 32
CK = 384
NK = -(-(1088 + BR - 1) // CK)
NC = 512
NN = D // NC
NT = 2 * NN
READY = 11


class Place:
    def __init__(self):
        self.g = lax.axis_index("grp")
        self.c = lax.axis_index("ctx")
        self.y = self.g // 2
        self.xl = self.g % 2
        self.z = self.c // 4
        self.xh = (self.c // 2) % 2
        self.co = self.c % 2
        self.xh2 = (self.xh + self.co) % 2

    def group(self, dy, flip):
        return ((self.y + dy) % 4) * 2 + (self.xl + flip) % 2

    def peer(self, dy, flip):
        ctx = self.z * 4 + self.xh2 * 2 + self.co if flip else self.c
        return (self.group(dy, flip), ctx)

    def level(self, z):
        return (self.g, z * 4 + self.xh * 2 + self.co)

    def quarter(self, b):
        xh = jnp.where((b % 2) == self.xl, self.xh, self.xh2)
        return xh * 2 + self.co


PEERS = [(dy, flip) for dy in range(4) for flip in range(2)][1:]


def rcopy(src, dst, ssem, rsem, device):
    return pltpu.make_async_remote_copy(
        src_ref=src, dst_ref=dst, send_sem=ssem, recv_sem=rsem, device_id=device, device_id_type=MESH
    )


def take(ref, sem):
    pltpu.make_async_copy(ref, ref, sem).wait()


def greet(devices):
    barrier = pltpu.get_barrier_semaphore()
    for device in devices:
        pl.semaphore_signal(barrier, inc=1, device_id=device, device_id_type=MESH)
    pl.semaphore_wait(barrier, len(devices))


def row_slots(place, groups, rows, offset, lens, adap, aslot):
    lane = lax.broadcasted_iota(jnp.int32, (8, len(groups) * rows), 1)
    out = jnp.zeros(lane.shape, jnp.int32)
    for i, b in enumerate(groups):
        pos = 64 * (place.z * 4 + place.quarter(b)) + offset + lane - i * rows
        mine = (lane >= i * rows) & (lane < (i + 1) * rows)
        end = jnp.int32(0)
        for r in range(REQS):
            begin = end
            end = begin + lens[b, r]
            hit = mine & (pos >= begin) & (pos < end)
            out = jnp.where(hit, aslot[adap[b, r]], out)
    return out[0:1, :]


def layer_kernel(
    lens, adap, aslot, tok, wq, wk, wv, w_out, dn_hbm, uq, ukv, do, uo_hbm, freq,
    out,
    xall, w, wo, dn, uo, acc, accm, uq_all, uk_all, uv_all, do_all, midsend, mid_all, qbuf, kvbuf,
    cosb, sinb, q_all, kv_all, att_buf, att_all, omsend, om_recv, om, pbuf, xrecv, sbuf, far, tup, tdn, rup, rdn,
    lsem, sent, tr, rr, mr, zr, gr, ar, orr, xr, yr,
):
    pc = Place()
    z = pc.z
    partner = pc.peer(0, 1)
    up = pc.peer(1, 0)
    down = pc.peer(3, 0)
    mate = (pc.g, z * 4 + pc.xh * 2 + 1 - pc.co)
    across = (pc.g, z * 4 + (1 - pc.xh) * 2 + pc.co)
    qcols = pl.ds(pl.multiple_of(pc.g * QC, QC), QC)
    kcols = pl.ds(pl.multiple_of(pc.g * KVC, KVC), KVC)

    local = [(tok.at[h * HR : (h + 1) * HR, :], xall.at[h, pc.g]) for h in range(H)] + [
        (wq, w.at[:, 0:QC]),
        (wk, w.at[:, QC : QC + KVC]),
        (wv, w.at[:, QC + KVC : QC + 2 * KVC]),
        (dn_hbm, dn),
        (uq.at[:, qcols], uq_all.at[pc.g]),
        (ukv.at[0, :, kcols], uk_all.at[pc.g]),
        (ukv.at[1, :, kcols], uv_all.at[pc.g]),
        (do.at[:, qcols], do_all.at[pc.g]),
        (uo_hbm, uo.at[pc.xl]),
        (w_out, wo),
    ]
    loads = [pltpu.make_async_copy(src, dst, lsem.at[i]) for i, (src, dst) in enumerate(local)]
    for load in loads:
        load.start()

    greet(
        [pc.peer(*p) for p in PEERS]
        + [pc.level((z + d) % 8) for d in range(1, 8)]
        + [mate, across]
    )

    def part(J):
        return J // NCH, pl.ds(pl.multiple_of((J % NCH) * KCH, KCH), KCH)

    def block(J, group):
        h, cols = part(J)
        return xall.at[h, group, :, cols]

    def own_copies(J):
        src = dst = block(J, pc.g)
        return (
            rcopy(src, dst, sent.at[0], rr.at[J, 0], up),
            rcopy(src, dst, sent.at[0], rr.at[J, 1], down),
            rcopy(src, dst, sent.at[0], rr.at[J, 3], partner),
        )

    def forward(J, group, wave, device):
        ref = block(J, group)
        return rcopy(ref, ref, sent.at[0], rr.at[J, wave], device)

    def arrived(J, wave, blocks=1):
        h, cols = part(J)
        take(xall.at[h, 0:blocks, :, cols], rr.at[J, wave])

    g_dn, g_up = pc.group(3, 0), pc.group(1, 0)

    def own(J):
        for copy in own_copies(J):
            copy.start()

    def stage_a(J):
        even = J % 2 == 0
        arrived(J, 0)

        @pl.when(even)
        def _():
            forward(J, g_dn, 3, partner).start()
            forward(J, g_dn, 3, up).start()

        @pl.when(J % 2 == 1)
        def _():
            forward(J, g_dn, 2, partner).start()

        arrived(J, 1)

        @pl.when(even)
        def _():
            forward(J, g_up, 2, partner).start()

        @pl.when(J % 2 == 1)
        def _():
            forward(J, g_up, 3, partner).start()
            forward(J, g_up, 3, down).start()

    def stage_b(J):
        arrived(J, 2)

        @pl.when(J % 2 == 0)
        def _():
            forward(J, pc.group(1, 1), 3, down).start()

        @pl.when(J % 2 == 1)
        def _():
            forward(J, pc.group(3, 1), 3, up).start()

    def stage_c(J):
        arrived(J, 3, 4)
        h, cols = part(J)
        even = h % 2
        x = xall[h, :, :, cols].reshape(NR, KCH)

        @pl.when(J % NCH == 0)
        def _():
            acc[even] = jnp.zeros(acc.shape[1:], F32)
            accm[even] = jnp.zeros(accm.shape[1:], F32)

        accm[even] += lax.dot_general(
            dn[:, cols], x, (((1,), (1,)), ((), ())), preferred_element_type=F32
        )
        acc[even] += jnp.dot(x, w[cols, :], preferred_element_type=F32)

    def table_copies(k, dy, flip):
        device = pc.peer(dy, flip)
        i = pc.group(dy, flip)
        qc = pl.ds(pl.multiple_of(i * QC, QC), QC)
        kc = pl.ds(pl.multiple_of(i * KVC, KVC), KVC)
        return (
            rcopy(uq.at[:, qc], uq_all.at[pc.g], sent.at[1], tr.at[0], device),
            rcopy(ukv.at[0, :, kc], uk_all.at[pc.g], sent.at[2], tr.at[1], device),
            rcopy(ukv.at[1, :, kc], uv_all.at[pc.g], sent.at[3], tr.at[2], device),
        )

    def late_copies():
        copies = [rcopy(uo_hbm, uo.at[pc.xl], sent.at[5], tr.at[4], partner)]
        for k, (dy, flip) in enumerate(PEERS):
            i = pc.group(dy, flip)
            qc = pl.ds(pl.multiple_of(i * QC, QC), QC)
            copies.append(
                rcopy(do.at[:, qc], do_all.at[pc.g], sent.at[4], tr.at[3], pc.peer(dy, flip))
            )
        return copies

    sub = lax.broadcasted_iota(jnp.int32, (HR, HD), 0)
    low = lax.broadcasted_iota(jnp.int32, (HR, HD), 1) < HD // 2

    def rotation(h, b):
        pos = 64 * (z * 4 + pc.quarter(b)) + HR * h + sub
        begin = jnp.zeros((HR, HD), jnp.int32)
        end = jnp.int32(0)
        for r in range(REQS):
            length = lens[b, r]
            end = end + length
            begin = begin + jnp.where(pos >= end, length, 0)
        angle = (pos - begin).astype(F32) * freq[...]
        rows = pl.ds(pl.multiple_of(h * NR + b * HR, HR), HR)
        cosb[rows, :] = jnp.cos(angle)
        sine = jnp.sin(angle)
        sinb[rows, :] = jnp.where(low, -sine, sine)

    def mid_copies(h):
        return [
            rcopy(midsend.at[h], mid_all.at[h, pc.g], sent.at[6], mr.at[h], pc.peer(*p))
            for k, p in enumerate(PEERS)
        ]

    def finish_mid(h):
        keep = (row_slots(pc, range(8), HR, HR * h, lens, adap, aslot) == pc.g).astype(F32)
        mid = (accm[h % 2] * keep).astype(BF16).reshape(3, RK, NR)
        midsend[h] = mid
        mid_all[h, pc.g] = mid
        for copy in mid_copies(h):
            copy.start()

    def kv_row(zsrc, quarter, h):
        return (zsrc * 4 + quarter) * H + h

    def z_copies(h, d):
        zd = (z + d) % 8
        device = pc.level(zd)
        return (
            rcopy(kvbuf.at[h, zd], kv_all.at[kv_row(z, pc.quarter(zd), h)], sent.at[7], zr.at[h], device),
            rcopy(qbuf.at[h, zd], q_all.at[z, h], sent.at[8], zr.at[H], device),
        )

    def finish_rows(h):
        take(mid_all.at[h, 0:7], mr.at[h])
        even = h % 2
        rows = pl.ds(pl.multiple_of(h * NR, NR), NR)
        cosv, sinv = cosb[rows, :], sinb[rows, :]

        def widen(which, table, base):
            mid = mid_all[h, :, which].reshape(8 * RK, NR)
            delta = lax.dot_general(
                mid, table[...].reshape(8 * RK, table.shape[2]), (((0,), (0,)), ((), ())),
                preferred_element_type=F32,
            )
            return base + 2.0 * delta

        def rope(v):
            return v * cosv + pltpu.roll(v, HD // 2, 1) * sinv

        key = rope(widen(1, uk_all, acc[even, :, QC : QC + KVC]))
        kvbuf[h, :, :, 0:HD] = key.astype(BF16).reshape(8, HR, HD)
        value = widen(2, uv_all, acc[even, :, QC + KVC : QC + 2 * KVC])
        kvbuf[h, :, :, HD : 2 * HD] = value.astype(BF16).reshape(8, HR, HD)
        kv_all[kv_row(z, q_own, h)] = kvbuf[h, z]
        for d in (4, 3, 5, 2, 6, 1, 7):
            z_copies(h, d)[0].start()
        query = widen(0, uq_all, acc[even, :, 0:QC])
        for j in range(4):
            qbuf[h, :, :, j * HD : (j + 1) * HD] = (
                rope(query[:, j * HD : (j + 1) * HD]).astype(BF16).reshape(8, HR, HD)
            )
        q_all[z, h] = qbuf[h, z]
        for d in (4, 3, 5, 2, 6, 1, 7):
            z_copies(h, d)[1].start()

    q_own = pc.quarter(z)
    q_across = (1 - q_own // 2) * 2 + pc.co
    xh_mate = jnp.where((z % 2) == pc.xl, pc.xh, (pc.xh + 1 - pc.co) % 2)
    q_mate = xh_mate * 2 + 1 - pc.co
    q_mate_across = (1 - xh_mate) * 2 + 1 - pc.co

    def kv_copy(quarter, h, d, k, device):
        ref = kv_all.at[kv_row((z + 8 - d) % 8, quarter, h)]
        return rcopy(ref, ref, sent.at[9], gr.at[jnp.where(k == 1, h, H + k // 2)], device)

    def spread_own(h):
        take(kv_all.at[0:7], zr.at[h])

        def one(d, carry):
            kv_copy(q_own, h, d, 1, across).start()
            kv_copy(q_own, h, d, 0, mate).start()
            return carry

        lax.fori_loop(0, 8, one, None)

    def spread_across(h):
        take(kv_all.at[0:8], gr.at[h])

        def one(d, carry):
            kv_copy(q_across, h, d, 2, mate).start()
            return carry

        lax.fori_loop(0, 8, one, None)

    def due(t, lag, run):
        last = t - lag

        @pl.when((last >= 0) & (last < NJ) & (last % NCH == NCH - 1))
        def _():
            run(last // NCH)

    def step(t, carry=None):
        @pl.when(t + LEAD < NJ)
        def _():
            own(t + LEAD)

        @pl.when(t < NJ)
        def _():
            stage_a(t)

        @pl.when((t >= LAG_B) & (t < NJ + LAG_B))
        def _():
            stage_b(t - LAG_B)

        @pl.when(t < NJ)
        def _():
            for i in range(8 // NCH):
                rotation(t // NCH, (t % NCH) * (8 // NCH) + i)

        @pl.when(t == LAG_C)
        def _():
            for i, table in enumerate((uq_all, uk_all, uv_all)):
                take(table.at[0:7], tr.at[i])

        @pl.when((t >= LAG_C) & (t < NJ + LAG_C))
        def _():
            stage_c(t - LAG_C)

        due(t, LAG_C, finish_mid)
        due(t, LAG_ROWS, finish_rows)
        due(t, LAG_OWN, spread_own)
        due(t, LAG_ACROSS, spread_across)
        return carry

    for load in loads[:H]:
        load.wait()
    for J in range(LEAD):
        own(J)
    for k, p in enumerate(PEERS):
        for copy in table_copies(k, *p):
            copy.start()
    for load in loads[H:]:
        load.wait()
    lax.fori_loop(0, NJ + LAG_ACROSS, step, None)
    for copy in late_copies():
        copy.start()

    take(q_all.at[0:7], zr.at[H])
    for k in range(2):
        take(kv_all.at[0 : 8 * H], gr.at[H + k])

    col = lax.broadcasted_iota(jnp.int32, (4 * BR, CK), 1)
    row1 = lax.broadcasted_iota(jnp.int32, (4 * BR, 1), 0) % BR
    scale = math.log2(math.e) / math.sqrt(HD)
    bk = CK // HR

    def offset_of(k):
        return 4 + jnp.where(k % 2 == 0, k // 2, -((k + 1) // 2))

    def back_copy(half, k):
        zd = (z + offset_of(k)) % 8
        return rcopy(att_buf.at[half, zd], att_all.at[half, z // 2, z % 2], sent.at[10], ar.at[half], pc.level(zd))

    def attend(it, carry):
        half, k = it // 8, it % 8
        zq = (z + offset_of(k)) % 8
        first = 64 * (zq * 4 + q_own) + BR * half
        pos = first + row1
        begin = jnp.zeros((4 * BR, 1), jnp.int32)
        end = jnp.int32(0)
        for r in range(REQS):
            length = lens[z, r]
            end = end + length
            begin = begin + jnp.where(pos >= end, length, 0)
        q = q_all[zq, pl.ds(half * (BR // HR), BR // HR)].reshape(BR, QC)
        q = jnp.concatenate([q[:, j * HD : (j + 1) * HD] for j in range(4)], axis=0)

        start = jnp.maximum(first + BR - NK * CK, 0)
        scores = []
        for i in range(NK):
            keys = kv_all[pl.ds(start // HR + i * bk, bk), :, 0:HD].reshape(CK, HD)
            s = lax.dot_general(q, keys, (((1,), (1,)), ((), ())), preferred_element_type=F32) * scale
            at = col + (start + i * CK)
            scores.append(jnp.where((at >= begin) & (at <= pos), s, NEG))
        top = functools.reduce(jnp.maximum, [jnp.max(s, axis=1, keepdims=True) for s in scores])
        total = jnp.zeros((4 * BR, 1), F32)
        accum = jnp.zeros((4 * BR, HD), F32)
        for i, s in enumerate(scores):
            values = kv_all[pl.ds(start // HR + i * bk, bk), :, HD : 2 * HD].reshape(CK, HD)
            p = jnp.exp2(s - top)
            total += jnp.sum(p, axis=1, keepdims=True)
            accum += jnp.dot(p.astype(BF16), values, preferred_element_type=F32)
        result = (accum / total).astype(BF16)
        for j in range(4):
            att_buf[half, zq, :, j * HD : (j + 1) * HD] = result[j * BR : (j + 1) * BR]

        @pl.when(k < 7)
        def _():
            back_copy(half, k).start()

        @pl.when(k == 7)
        def _():
            att_all[half, z // 2, z % 2] = att_buf[half, z]

        return carry

    def om_copy(half, k, dy, flip):
        to = pc.group(dy, flip)
        return rcopy(
            omsend.at[half, to % 2, to // 2], om_recv.at[half, pc.g], sent.at[11], orr.at[half],
            pc.peer(dy, flip),
        )

    def mid_send(half):
        for column in range(2):
            rows = att_all[half, :, column].reshape(4 * BR, QC)
            omsend[half, column] = lax.dot_general(
                do_all[...].reshape(8 * RK, QC), rows, (((1,), (1,)), ((), ())), preferred_element_type=F32
            ).reshape(4, 2 * RK, 4 * BR)
        for k, p in enumerate(PEERS):
            om_copy(half, k, *p).start()
        om_recv[half, pc.g] = omsend[half, pc.xl, pc.y]

    def mid_done(half):
        groups = [b * 2 + pc.xl for b in range(4)]
        slots = row_slots(pc, groups, BR, BR * half, lens, adap, aslot)
        mine = 2 * pc.y + lax.broadcasted_iota(jnp.int32, (2 * RK, 4 * BR), 0) // RK
        keep = (slots == mine).astype(F32)
        take(om_recv.at[half, 0:7], orr.at[half])
        om[half] = (jnp.sum(om_recv[half], axis=0) * keep).astype(BF16)

    def att_ready(half):
        take(att_buf.at[half, 0:7], ar.at[half])

    y_far, y_up, y_dn = (pc.y + 2) % 4, (pc.y + 1) % 4, (pc.y + 3) % 4

    def x_copy(J):
        return rcopy(pbuf.at[J, :, 1 - pc.xl], xrecv.at[J], sent.at[12], xr.at[J // 2], partner)

    def far_copy(J, odd):
        return rcopy(sbuf.at[J, y_far], far.at[J], sent.at[13], yr.at[J // 2, 0], down if odd else up)

    def up_copy(J):
        return rcopy(tup.at[J], rup.at[J], sent.at[14], yr.at[J // 2, 1], up)

    def dn_copy(J):
        return rcopy(tdn.at[J], rdn.at[J], sent.at[15], yr.at[J // 2, 1], down)

    def stage_p(J):
        half = J // NN
        cols = pl.ds(pl.multiple_of((J % NN) * NC, NC), NC)
        rows = att_all[half].reshape(8 * BR, QC)
        total = jnp.dot(rows, wo[:, cols], preferred_element_type=F32)
        pbuf[J] = total.astype(BF16).reshape(4, 2, BR, NC)
        x_copy(J).start()

    def stage_s(J, odd):
        half = J // NN
        cols = pl.ds(pl.multiple_of((J % NN) * NC, NC), NC)
        delta = lax.dot_general(
            om[half], uo[:, :, cols].reshape(2 * RK, NC), (((0,), (0,)), ((), ())), preferred_element_type=F32
        ).reshape(4, BR, NC)
        total = pbuf[J, :, pc.xl].astype(F32) + xrecv[J].astype(F32) + 2.0 * delta
        sbuf[J] = total.astype(BF16)
        far_copy(J, odd).start()
        if odd:
            tup[J] = sbuf[J, y_up]
            up_copy(J).start()
        else:
            tdn[J] = sbuf[J, y_dn]
            dn_copy(J).start()

    def stage_t(J, odd):
        if odd:
            tdn[J] = (sbuf[J, y_dn].astype(F32) + far[J].astype(F32)).astype(BF16)
            dn_copy(J).start()
        else:
            tup[J] = (sbuf[J, y_up].astype(F32) + far[J].astype(F32)).astype(BF16)
            up_copy(J).start()

    def stage_f(J):
        half = J // NN
        cols = pl.ds(pl.multiple_of((J % NN) * NC, NC), NC)
        total = sbuf[J, pc.y].astype(F32) + rup[J].astype(F32) + rdn[J].astype(F32)
        out[pl.ds(pl.multiple_of(half * BR, BR), BR), cols] = total.astype(BF16)

    HP = NN // 2

    def pair_p(u):
        stage_p(2 * u)
        stage_p(2 * u + 1)

    def attend_and_project(it, carry):
        attend(it, carry)

        @pl.when(it == READY)
        def _():
            take(do_all.at[0:7], tr.at[3])
            take(uo.at[0], tr.at[4])
            att_ready(0)
            mid_send(0)

        @pl.when((it >= READY) & (it < READY + 4))
        def _():
            for i in range(HP // 4):
                pair_p((it - READY) * (HP // 4) + i)

        return carry

    lax.fori_loop(0, 16, attend_and_project, None)
    mid_done(0)

    def reduce(t, carry):
        @pl.when(t == HP)
        def _():
            mid_done(1)

        @pl.when(t < 2 * HP)
        def _():
            take(xrecv.at[0:2], xr.at[t])
            stage_s(2 * t, False)
            stage_s(2 * t + 1, True)

        @pl.when((t >= 1) & (t < 2 * HP + 1))
        def _():
            take(far.at[0:2], yr.at[t - 1, 0])
            stage_t(2 * t - 2, False)
            stage_t(2 * t - 1, True)

        @pl.when(t >= 2)
        def _():
            take(rup.at[0:4], yr.at[t - 2, 1])
            stage_f(2 * t - 4)
            stage_f(2 * t - 3)

        @pl.when(t == 1)
        def _():
            att_ready(1)
            mid_send(1)
            pair_p(HP)

        @pl.when((t >= 1) & (t < HP))
        def _():
            pair_p(t + HP)

        return carry

    lax.fori_loop(0, 2 * HP + 2, reduce, None)

    for i, ref in enumerate(
        (
            xall.at[:, 0:7], uq_all.at[0:7], uk_all.at[0:7], uv_all.at[0:7], do_all.at[0:7], uo.at[0],
            mid_all.at[:, 0:7], kvbuf.at[:, 0:7], qbuf.at[:, 0:7], kv_all.at[0 : 24 * H],
            att_buf.at[:, 0:7], om_recv.at[:, 0:7], xrecv, far, rup, rdn,
        )
    ):
        take(ref, sent.at[i])


def layer(*args):
    any_ = pl.BlockSpec(memory_space=pltpu.HBM)
    vmem = pl.BlockSpec(memory_space=pltpu.VMEM)
    smem = pl.BlockSpec(memory_space=pltpu.SMEM)
    dma = pltpu.SemaphoreType.DMA
    return pl.pallas_call(
        layer_kernel,
        name="layer",
        out_shape=jax.ShapeDtypeStruct((64, D), BF16),
        in_specs=[smem] * 3 + [any_] * 10 + [vmem],
        out_specs=vmem,
        scratch_shapes=[
            pltpu.VMEM((H, 8, HR, D), BF16),
            pltpu.VMEM((D, QC + 2 * KVC), BF16),
            pltpu.VMEM((QC, D), BF16),
            pltpu.VMEM((3 * RK, D), BF16),
            pltpu.VMEM((2, RK, D), BF16),
            pltpu.VMEM((2, NR, QC + 2 * KVC), F32),
            pltpu.VMEM((2, 3 * RK, NR), F32),
            pltpu.VMEM((8, RK, QC), BF16),
            pltpu.VMEM((8, RK, KVC), BF16),
            pltpu.VMEM((8, RK, KVC), BF16),
            pltpu.VMEM((8, RK, QC), BF16),
            pltpu.VMEM((H, 3, RK, NR), BF16),
            pltpu.VMEM((H, 8, 3, RK, NR), BF16),
            pltpu.VMEM((H, 8, HR, QC), BF16),
            pltpu.VMEM((H, 8, HR, 2 * HD), BF16),
            pltpu.VMEM((512, HD), F32),
            pltpu.VMEM((512, HD), F32),
            pltpu.VMEM((8, H, HR, QC), BF16),
            pltpu.VMEM((32 * H, HR, 2 * HD), BF16),
            pltpu.VMEM((2, 8, BR, QC), BF16),
            pltpu.VMEM((2, 4, 2, BR, QC), BF16),
            pltpu.VMEM((2, 2, 4, 2 * RK, 4 * BR), F32),
            pltpu.VMEM((2, 8, 2 * RK, 4 * BR), F32),
            pltpu.VMEM((2, 2 * RK, 4 * BR), BF16),
            pltpu.VMEM((NT, 4, 2, BR, NC), BF16),
            pltpu.VMEM((NT, 4, BR, NC), BF16),
            pltpu.VMEM((NT, 4, BR, NC), BF16),
            pltpu.VMEM((NT, BR, NC), BF16),
            pltpu.VMEM((NT, BR, NC), BF16),
            pltpu.VMEM((NT, BR, NC), BF16),
            pltpu.VMEM((NT, BR, NC), BF16),
            pltpu.VMEM((NT, BR, NC), BF16),
            dma((10 + H,)),
            dma((16,)),
            dma((5,)),
            dma((NJ, 4)),
            dma((H,)),
            dma((H + 1,)),
            dma((H + 2,)),
            dma((2,)),
            dma((2,)),
            dma((NT // 2,)),
            dma((NT // 2, 2)),
        ],
        compiler_params=pltpu.CompilerParams(
            collective_id=0, has_side_effects=True, vmem_limit_bytes=61 << 20
        ),
    )(*args)


def body(
    tokens, req_lengths, req_adapter, adapter_slot, query_weight, key_weight, value_weight, w_out,
    down_qkv, up_query, up_kv, down_out, up_out,
):
    half = np.arange(HD) % (HD // 2)
    freq = jnp.asarray(np.exp(half * (-2.0 * math.log(ROPE_BASE) / HD)).astype(np.float32)[None, :])
    out = layer(
        req_lengths, req_adapter, adapter_slot, tokens[0], query_weight, key_weight, value_weight, w_out,
        down_qkv[0], up_query[0], up_kv[0], down_out[0], up_out[0], freq,
    )
    return out[None]


def solution(mesh):
    placed = (
        P("grp", "ctx", None),
        P(),
        P(),
        P(),
        P(None, "grp"),
        P(None, "grp"),
        P(None, "grp"),
        P("grp", None),
        P("grp", None, None),
        P("grp", None, None),
        P("grp", None, None, None),
        P("grp", None, None),
        P("grp", None, None),
    )
    return jax.shard_map(
        body, mesh=mesh, in_specs=placed, out_specs=P("grp", "ctx", None), check_vma=False
    )
```
